32 devices in a mesh: fsdp: 8 (over y, x, core), head: 4 (over z).
Axes of the slice: x: 2, y: 2, z: 4, core: 2. Of those that a mesh axis runs over, the one named last changes fastest.
Arguments:
- query_nope: float32 [2048, 2048], P('fsdp', 'head'), may hold values from -6 to 6
- query_rope: float32 [2048, 1024], P('fsdp', 'head'), may hold values from -12 to 12
- latent: float32 [2048, 512], P(('fsdp', 'head')), may hold values from -6 to 6
- rope_key: float32 [2048, 64], P(('fsdp', 'head')), may hold values from -4 to 4
- cotangent: float32 [2048, 2048], P('fsdp', 'head'), may hold values from -6 to 6
- bounds: int32 [8, 2], P('fsdp'), may hold values from 1 to 256, as said below
- key_up: float32 [512, 2048], P('fsdp', 'head'), may hold values from -0.25 to 0.25
- value_up: float32 [512, 2048], P('fsdp', 'head'), may hold values from -0.25 to 0.25
Outputs:
- query_nope_grad: float32 [2048, 2048], P('fsdp', 'head')
- query_rope_grad: float32 [2048, 1024], P('fsdp', 'head')
- latent_grad: float32 [2048, 512], P(('fsdp', 'head'))
- rope_key_grad: float32 [2048, 64], P(('fsdp', 'head'))
- key_up_grad: float32 [512, 2048], P('fsdp', 'head')
- value_up_grad: float32 [512, 2048], P('fsdp', 'head')
The draws below stay inside these ranges and needn't reach their ends.
Inputs may be any that keep to these rules, and one draw needn't show every extreme that they name: bounds[s, 0] is the length of sequence s's image prefix, attended in both directions, and bounds[s, 1] its number of valid tokens; 1 <= bounds[s, 0] < 128 < bounds[s, 1]; some sequence has all 256 tokens valid.
All inputs are finite; a program needn't handle non-finite values.
Results may differ from the reference program's by a relative error of at most 0.0003.
Values sent between devices are 32-bit elements; how exact they have to be, the bound alone decides.
No kernel may reach another device: no remote copies, remote signals or barrier semaphores. Data moves between devices by JAX's collectives and lax.ppermute only.
A program may use at most 64 MiB of HBM per device.

```python
import jax
import jax.numpy as jnp
from jax import lax

LAT = 512
NOPE = 128
ROPE = 64
VHEAD = 128
SEQ = 256
HEADS = 16
SEQS = 8
TOKENS = 2048


def draw_rope_key(key, part):
    rough = jax.random.truncated_normal(jax.random.fold_in(key, 17), -4.0, 4.0, (TOKENS, ROPE), jnp.float32)
    return rough


def draw_query_rope(key, part):
    rough = jax.random.truncated_normal(jax.random.fold_in(key, 29), -4.0, 4.0, (TOKENS, HEADS, ROPE), jnp.float32)
    return rough.reshape(TOKENS, HEADS * ROPE)


def draw_bounds(key, part):
    prefix = jax.random.randint(jax.random.fold_in(key, 3), (SEQS,), 1, SEQ // 2)
    valid = jax.random.randint(jax.random.fold_in(key, 5), (SEQS,), SEQ // 2 + 2, SEQ + 1)
    valid = jnp.where(jnp.arange(SEQS) == 0, SEQ, valid)
    return jnp.stack([prefix, valid], axis=1).astype(jnp.int32)


def block_scale(rng, extent, cuts, low, top_value):
    factor_of = 1.0
    for dim, shards_of in cuts:
        heights = jax.random.uniform(jax.random.fold_in(jax.random.fold_in(rng, 6), dim), (shards_of,), jnp.float32, low / len(cuts), top_value / len(cuts))
        factor_of = factor_of * jnp.repeat(jnp.exp(heights), extent[dim] // shards_of).reshape((-1,) + (1,) * (len(extent) - 1 - dim))
    return factor_of


def bell_draw(stream_key, dims, scale, most, pieces=(), kind=jnp.bfloat16):
    result = scale * jax.random.normal(stream_key, dims, jnp.float32)
    if pieces:
        result = result * block_scale(stream_key, dims, pieces, -0.22, 0.18)
    return jnp.clip(result, -most, most).astype(kind)


def setup_inputs(seed: int = 0) -> dict:
    arg_keys = jax.random.split(jax.random.key(seed), 9)
    return {
        "query_nope": bell_draw(arg_keys[0], (TOKENS, HEADS * NOPE), 1.0, 6.0, ((0, 8), (1, 4)), jnp.float32),
        "query_rope": draw_query_rope(jax.random.fold_in(arg_keys[8], 71), 0),
        "latent": bell_draw(arg_keys[2], (TOKENS, LAT), 1.0, 6.0, ((0, 32),), jnp.float32),
        "rope_key": draw_rope_key(jax.random.fold_in(arg_keys[8], 71), 0),
        "cotangent": bell_draw(arg_keys[4], (TOKENS, HEADS * VHEAD), 1.0, 6.0, ((0, 8), (1, 4)), jnp.float32),
        "bounds": draw_bounds(jax.random.fold_in(arg_keys[8], 71), 0),
        "key_up": bell_draw(arg_keys[6], (LAT, HEADS * NOPE), LAT ** -0.5, 0.25, ((0, 8), (1, 4)), jnp.float32),
        "value_up": bell_draw(arg_keys[7], (LAT, HEADS * VHEAD), LAT ** -0.5, 0.25, ((0, 8), (1, 4)), jnp.float32),
    }


HIGHEST = lax.Precision.HIGHEST


def visible_mask(limits, length):
    position = jnp.arange(length)
    query_pos = position[:, None]
    key_pos = position[None, :]
    return (key_pos < limits[1]) & ((key_pos <= query_pos) | (key_pos < limits[0]))


def attention_grads(query_nope, query_rope, key_rows, value_rows, shared_rows, cotangent, limits):
    length = query_nope.shape[0]
    head_count = query_nope.shape[1] // NOPE
    query_nope = query_nope.reshape(length, head_count, NOPE)
    query_rope = query_rope.reshape(length, head_count, ROPE)
    key_rows = key_rows.reshape(length, head_count, NOPE)
    value_rows = value_rows.reshape(length, head_count, VHEAD)
    cotangent = cotangent.reshape(length, head_count, VHEAD)
    factor = (NOPE + ROPE) ** -0.5
    scores = jnp.einsum("ihd,jhd->hij", query_nope, key_rows, precision=HIGHEST)
    scores = (scores + jnp.einsum("ihr,jr->hij", query_rope, shared_rows, precision=HIGHEST)) * factor
    scores = jnp.where(visible_mask(limits, length)[None], scores, -jnp.inf)
    attend = jax.nn.softmax(scores, axis=-1)
    outputs = jnp.einsum("hij,jhv->ihv", attend, value_rows, precision=HIGHEST)
    row_dot = jnp.sum(cotangent * outputs, axis=-1)
    value_grad = jnp.einsum("hij,ihv->jhv", attend, cotangent, precision=HIGHEST)
    grad_attend = jnp.einsum("ihv,jhv->hij", cotangent, value_rows, precision=HIGHEST)
    grad_scores = attend * (grad_attend - jnp.transpose(row_dot)[:, :, None]) * factor
    nope_grad = jnp.einsum("hij,jhd->ihd", grad_scores, key_rows, precision=HIGHEST)
    rope_grad = jnp.einsum("hij,jr->ihr", grad_scores, shared_rows, precision=HIGHEST)
    key_grad = jnp.einsum("hij,ihd->jhd", grad_scores, query_nope, precision=HIGHEST)
    shared_grad = jnp.einsum("hij,ihr->jr", grad_scores, query_rope, precision=HIGHEST)
    return (nope_grad.reshape(length, head_count * NOPE), rope_grad.reshape(length, head_count * ROPE),
            key_grad.reshape(length, head_count * NOPE), value_grad.reshape(length, head_count * VHEAD), shared_grad)


def reference(query_nope, query_rope, latent, rope_key, cotangent, bounds, key_up, value_up):
    seq_count = bounds.shape[0]

    def one_sequence(carry, items):
        nope_rows, rope_rows, latent_rows, shared_rows, cot_rows, limits = items
        key_rows = jnp.dot(latent_rows, key_up, precision=HIGHEST, preferred_element_type=jnp.float32)
        value_rows = jnp.dot(latent_rows, value_up, precision=HIGHEST, preferred_element_type=jnp.float32)
        nope_grad, rope_grad, key_grad, value_grad, shared_grad = attention_grads(
            nope_rows, rope_rows, key_rows, value_rows, shared_rows, cot_rows, limits)
        latent_grad = jnp.dot(key_grad, key_up.T, precision=HIGHEST, preferred_element_type=jnp.float32)
        latent_grad = latent_grad + jnp.dot(value_grad, value_up.T, precision=HIGHEST, preferred_element_type=jnp.float32)
        key_total = carry[0] + jnp.dot(latent_rows.T, key_grad, precision=HIGHEST, preferred_element_type=jnp.float32)
        value_total = carry[1] + jnp.dot(latent_rows.T, value_grad, precision=HIGHEST, preferred_element_type=jnp.float32)
        return (key_total, value_total), (nope_grad, rope_grad, latent_grad, shared_grad)

    items = (query_nope.reshape(seq_count, SEQ, -1), query_rope.reshape(seq_count, SEQ, -1),
             latent.reshape(seq_count, SEQ, -1), rope_key.reshape(seq_count, SEQ, -1),
             cotangent.reshape(seq_count, SEQ, -1), bounds)
    start_sums = (jnp.zeros(key_up.shape, jnp.float32), jnp.zeros(value_up.shape, jnp.float32))
    totals, stacked = lax.scan(one_sequence, start_sums, items)
    return (stacked[0].reshape(seq_count * SEQ, -1), stacked[1].reshape(seq_count * SEQ, -1),
            stacked[2].reshape(seq_count * SEQ, -1), stacked[3].reshape(seq_count * SEQ, -1),
            totals[0], totals[1])
```

```python
import functools

import jax
import jax.numpy as jnp
from jax import lax
from jax.experimental import pallas as pl
from jax.experimental.pallas import tpu as pltpu
from jax.sharding import PartitionSpec as P

NOPE = 128
ROPE = 64
VHEAD = 128
F32 = jnp.float32
BF16 = jnp.bfloat16
LANES = 128


def split(x):
    high = x.astype(BF16)
    return high, (x - high.astype(F32)).astype(BF16)


def product(left, right, left_dim, right_dim):
    dims = (((left_dim,), (right_dim,)), ((), ()))
    dot = functools.partial(lax.dot_general, dimension_numbers=dims, preferred_element_type=F32)
    return dot(left[0], right[0]) + (dot(left[0], right[1]) + dot(left[1], right[0]))


def columns(pair, start, size):
    return pair[0][:, start : start + size], pair[1][:, start : start + size]


def gather_kernel_body(refs, ways, chips, rows_up, place_ref, latent_all, key_all, value_all):
    latent_refs, up_refs = refs[:ways], refs[ways:]
    token_rows = latent_refs[0].shape[0]
    mine, row = place_ref[0], place_ref[1]
    for step in range(ways):
        owner = lax.rem(mine + (ways - step), ways)
        latent_all[pl.ds(pl.multiple_of(owner * token_rows, 8), token_rows), :] = latent_refs[step][...]
    for step in range(2 * chips):
        owner = jnp.bitwise_xor(row, step)
        at = pl.ds(pl.multiple_of(owner * rows_up, 8), rows_up)
        key_all[at, :] = up_refs[step][:rows_up, :]
        value_all[at, :] = up_refs[step][rows_up:, :]


def attention_kernel(ways, chips, lat, place_ref, limit_ref, *refs):
    count = ways + 2 * chips
    gathered, refs = refs[:count], refs[count:]
    (nope_ref, rope_ref, cot_ref, nope_out, rope_out, latent_out, keep_out, send_out,
     latent_all, key_all, value_all, up_grad) = refs
    rows_up = gathered[ways].shape[0] // 2
    gather_kernel_body(gathered, ways, chips, rows_up, place_ref, latent_all, key_all, value_all)
    length, width = nope_ref.shape
    head_count = width // NOPE
    factor = (NOPE + ROPE) ** (-0.5)

    latent = split(latent_all[:, :lat])
    shared = split(latent_all[:, lat : lat + ROPE])
    key_up, value_up = split(key_all[...]), split(value_all[...])
    key_rows = split(product(latent, key_up, 1, 0))
    value_rows = split(product(latent, value_up, 1, 0))

    query_pos = lax.broadcasted_iota(jnp.int32, (length, length), 0)
    key_pos = lax.broadcasted_iota(jnp.int32, (length, length), 1)
    visible = (key_pos < limit_ref[0, 1]) & ((key_pos <= query_pos) | (key_pos < limit_ref[0, 0]))

    key_grads, value_grads = [], []
    shared_grad = jnp.zeros((length, ROPE), F32)
    for head in range(head_count):
        nope = split(nope_ref[:, head * NOPE : (head + 1) * NOPE])
        rope = split(rope_ref[:, head * ROPE : (head + 1) * ROPE])
        cot = split(cot_ref[:, head * VHEAD : (head + 1) * VHEAD])
        keys = columns(key_rows, head * NOPE, NOPE)
        values = columns(value_rows, head * VHEAD, VHEAD)
        scores = (product(nope, keys, 1, 1) + product(rope, shared, 1, 1)) * factor
        scores = jnp.where(visible, scores, -jnp.inf)
        weight = jnp.exp(scores - jnp.max(scores, axis=1, keepdims=True))
        attend = weight / jnp.sum(weight, axis=1, keepdims=True)
        grad_attend = product(cot, values, 1, 1)
        row_dot = jnp.sum(attend * grad_attend, axis=1, keepdims=True)
        grad_scores = split(attend * (grad_attend - row_dot) * factor)
        attend = split(attend)
        value_grads.append(product(attend, cot, 0, 0))
        nope_out[:, head * NOPE : (head + 1) * NOPE] = product(grad_scores, keys, 1, 0)
        rope_out[:, head * ROPE : (head + 1) * ROPE] = product(grad_scores, shared, 1, 0)
        key_grads.append(product(grad_scores, nope, 0, 0))
        shared_grad = shared_grad + product(grad_scores, rope, 0, 0)
    key_grad = split(jnp.concatenate(key_grads, axis=1))
    value_grad = split(jnp.concatenate(value_grads, axis=1))
    latent_term = product(key_grad, key_up, 1, 1) + product(value_grad, value_up, 1, 1)

    token_rows = length // ways
    latent_all[:, :lat] = latent_term
    latent_all[:, lat : lat + ROPE] = shared_grad
    mine, row = place_ref[0], place_ref[1]
    for step in range(ways):
        owner = lax.rem(mine + step, ways)
        latent_out[step, :, :] = latent_all[pl.ds(pl.multiple_of(owner * token_rows, 8), token_rows), :]

    up_grad[:, :width] = product(latent, key_grad, 0, 0)
    up_grad[:, width:] = product(latent, value_grad, 0, 0)
    for step in range(chips):
        own = jnp.bitwise_xor(row, 2 * step)
        other = jnp.bitwise_xor(row, 2 * step + 1)
        keep_out[step, :, :] = up_grad[pl.ds(pl.multiple_of(own * rows_up, 8), rows_up), :]
        send_out[step, :, :] = up_grad[pl.ds(pl.multiple_of(other * rows_up, 8), rows_up), :]


def pack_kernel(latent_ref, rope_ref, key_ref, value_ref, tokens_out, ups_out):
    lat = latent_ref.shape[1]
    rows_up = key_ref.shape[0]
    tokens_out[:, :lat] = latent_ref[...]
    tokens_out[:, lat : lat + ROPE] = rope_ref[...]
    tokens_out[:, lat + ROPE :] = jnp.zeros((latent_ref.shape[0], tokens_out.shape[1] - lat - ROPE), F32)
    ups_out[:rows_up, :] = key_ref[...]
    ups_out[rows_up:, :] = value_ref[...]


def in_vmem(count):
    return [pl.BlockSpec(memory_space=pltpu.VMEM)] * count


def shape(*dims):
    return jax.ShapeDtypeStruct(dims, F32)


def on_device(fsdp, ways, query_nope, query_rope, latent, rope_key, cotangent, bounds, key_up, value_up):
    chips = fsdp // 2
    token_rows, lat = latent.shape
    rows_up, width = key_up.shape
    length = query_nope.shape[0]
    packed = -(-(lat + ROPE) // LANES) * LANES

    def swap(x, step):
        return lax.ppermute(x, "fsdp", [(i, i ^ step) for i in range(fsdp)])

    def shift(x, step):
        return lax.ppermute(x, "head", [(i, (i + step) % ways) for i in range(ways)])

    tokens, ups = pl.pallas_call(
        pack_kernel, out_shape=(shape(token_rows, packed), shape(2 * rows_up, width)),
        in_specs=in_vmem(4), out_specs=in_vmem(2),
    )(latent, rope_key, key_up, value_up)
    token_blocks = [tokens] + [shift(tokens, step) for step in range(1, ways)]
    even = [ups] + [swap(ups, 2 * step) for step in range(1, chips)]
    odd = [swap(block, 1) for block in even]
    up_blocks = [block for pair in zip(even, odd) for block in pair]

    place = jnp.stack([lax.axis_index("head"), lax.axis_index("fsdp")]).astype(jnp.int32)
    nope_grad, rope_grad, shares, keep, send = pl.pallas_call(
        functools.partial(attention_kernel, ways, chips, lat),
        out_shape=(
            shape(length, width), shape(*query_rope.shape), shape(ways, token_rows, packed),
            shape(chips, rows_up, 2 * width), shape(chips, rows_up, 2 * width),
        ),
        in_specs=[pl.BlockSpec(memory_space=pltpu.SMEM)] * 2 + in_vmem(ways + fsdp + 3),
        out_specs=in_vmem(5),
        scratch_shapes=[
            pltpu.VMEM((length, packed), F32), pltpu.VMEM((lat, width), F32), pltpu.VMEM((lat, width), F32),
            pltpu.VMEM((lat, 2 * width), F32),
        ],
    )(place, bounds, *token_blocks, *up_blocks, query_nope, query_rope, cotangent)

    both = keep + swap(send, 1)
    total = both[0]
    for step in range(1, chips):
        total = total + swap(both[step], 2 * step)
    share = shares[0]
    for step in range(1, ways):
        share = share + shift(shares[step], step)
    return (nope_grad, rope_grad, share[:, :lat], share[:, lat : lat + ROPE], total[:, :width], total[:, width:])


def solution(mesh):
    return jax.shard_map(
        functools.partial(on_device, mesh.shape["fsdp"], mesh.shape["head"]),
        mesh=mesh,
        in_specs=(
            P("fsdp", "head"),
            P("fsdp", "head"),
            P(("fsdp", "head"), None),
            P(("fsdp", "head"), None),
            P("fsdp", "head"),
            P("fsdp", None),
            P("fsdp", "head"),
            P("fsdp", "head"),
        ),
        out_specs=(
            P("fsdp", "head"),
            P("fsdp", "head"),
            P(("fsdp", "head"), None),
            P(("fsdp", "head"), None),
            P("fsdp", "head"),
            P("fsdp", "head"),
        ),
        check_vma=False,
    )
```

```python
import functools

import jax
import jax.numpy as jnp
from jax import lax
from jax.experimental import pallas as pl
from jax.experimental.pallas import tpu as pltpu
from jax.sharding import PartitionSpec as P

NOPE = 128
ROPE = 64
VHEAD = 128
F32 = jnp.float32
BF16 = jnp.bfloat16


HBM = pl.BlockSpec(memory_space=pltpu.HBM)
VMEM = pl.BlockSpec(memory_space=pltpu.VMEM)
SMEM = pl.BlockSpec(memory_space=pltpu.SMEM)


def split(x):
    high = x.astype(BF16)
    return high, (x - high.astype(F32)).astype(BF16)


def product(left, right, left_dim, right_dim):
    dims = (((left_dim,), (right_dim,)), ((), ()))
    dot = functools.partial(lax.dot_general, dimension_numbers=dims, preferred_element_type=F32)
    return dot(left[0], right[0]) + (dot(left[0], right[1]) + dot(left[1], right[0]))


def columns(pair, start, size):
    return pair[0][:, start : start + size], pair[1][:, start : start + size]


def rows_at(index, rows):
    return pl.ds(pl.multiple_of(index * rows, 8), rows)


def pack_tokens(rows, lat, out_ref, wide, narrow):
    folds = lat // ROPE
    fold = rows // folds
    out_ref[:rows, :] = wide
    for part in range(folds):
        out_ref[rows : rows + fold, part * ROPE : (part + 1) * ROPE] = narrow[part * fold : (part + 1) * fold, :]


def unpack_narrow(rows, lat, block):
    folds = lat // ROPE
    fold = rows // folds
    return jnp.concatenate([block[rows : rows + fold, part * ROPE : (part + 1) * ROPE] for part in range(folds)], axis=0)


def pack_kernel(latent_ref, rope_ref, key_ref, value_ref, tokens_out, ups_out, rope, sems):
    rows, lat = latent_ref.shape
    rows_up = key_ref.shape[0]
    copies = [
        pltpu.make_async_copy(rope_ref, rope, sems.at[0]),
        pltpu.make_async_copy(key_ref, ups_out.at[pl.ds(0, rows_up)], sems.at[1]),
        pltpu.make_async_copy(value_ref, ups_out.at[pl.ds(rows_up, rows_up)], sems.at[2]),
        pltpu.make_async_copy(latent_ref, tokens_out.at[pl.ds(0, rows)], sems.at[3]),
    ]
    for copy in copies:
        copy.start()
    copies[0].wait()
    folds = lat // ROPE
    fold = rows // folds
    for part in range(folds):
        tokens_out[rows : rows + fold, part * ROPE : (part + 1) * ROPE] = rope[part * fold : (part + 1) * fold, :]
    for copy in copies[1:]:
        copy.wait()


def attention_kernel(ways, chips, place_ref, limit_ref, *refs):
    token_refs, refs = refs[:ways], refs[ways:]
    up_refs, refs = refs[: 2 * chips], refs[2 * chips :]
    nope_hbm, rope_hbm, cot_hbm, nope_out, rope_out = refs[:5]
    share_refs, refs = refs[5 : 5 + ways], refs[5 + ways :]
    keep_refs, refs = refs[:chips], refs[chips:]
    (send_ref, latent_all, shared_all, key_all, value_all, up_grad,
     nope_ref, rope_ref, cot_ref, nope_grad, rope_grad, sems) = refs
    length, width = nope_ref.shape
    lat = latent_all.shape[1]
    rows = length // ways
    rows_up = up_refs[0].shape[0] // 2
    head_count = width // NOPE
    factor = (NOPE + ROPE) ** (-0.5)
    mine, row = place_ref[0], place_ref[1]

    loads = [
        pltpu.make_async_copy(nope_hbm, nope_ref, sems.at[0]),
        pltpu.make_async_copy(rope_hbm, rope_ref, sems.at[1]),
        pltpu.make_async_copy(cot_hbm, cot_ref, sems.at[2]),
    ]
    for copy in loads:
        copy.start()

    for step in range(ways):
        owner = lax.rem(mine + (ways - step), ways)
        block = token_refs[step][...]
        latent_all[rows_at(owner, rows), :] = block[:rows, :]
        shared_all[rows_at(owner, rows), :] = unpack_narrow(rows, lat, block)
    for step in range(2 * chips):
        at = rows_at(jnp.bitwise_xor(row, step), rows_up)
        key_all[at, :] = up_refs[step][:rows_up, :]
        value_all[at, :] = up_refs[step][rows_up:, :]

    latent, shared = split(latent_all[...]), split(shared_all[...])
    key_up, value_up = split(key_all[...]), split(value_all[...])
    key_rows = split(product(latent, key_up, 1, 0))
    value_rows = split(product(latent, value_up, 1, 0))

    query_pos = lax.broadcasted_iota(jnp.int32, (length, length), 0)
    key_pos = lax.broadcasted_iota(jnp.int32, (length, length), 1)
    visible = (key_pos < limit_ref[0, 1]) & ((key_pos <= query_pos) | (key_pos < limit_ref[0, 0]))
    for copy in loads:
        copy.wait()

    key_grads, value_grads, stores = [], [], []
    shared_grad = jnp.zeros((length, ROPE), F32)
    for head in range(head_count):
        nope = split(nope_ref[:, head * NOPE : (head + 1) * NOPE])
        rope = split(rope_ref[:, head * ROPE : (head + 1) * ROPE])
        cot = split(cot_ref[:, head * VHEAD : (head + 1) * VHEAD])
        keys = columns(key_rows, head * NOPE, NOPE)
        values = columns(value_rows, head * VHEAD, VHEAD)
        scores = (product(nope, keys, 1, 1) + product(rope, shared, 1, 1)) * factor
        scores = jnp.where(visible, scores, -jnp.inf)
        weight = jnp.exp(scores - jnp.max(scores, axis=1, keepdims=True))
        attend = weight / jnp.sum(weight, axis=1, keepdims=True)
        grad_attend = product(cot, values, 1, 1)
        row_dot = jnp.sum(attend * grad_attend, axis=1, keepdims=True)
        grad_scores = split(attend * (grad_attend - row_dot) * factor)
        attend = split(attend)
        value_grads.append(product(attend, cot, 0, 0))
        nope_grad[:, head * NOPE : (head + 1) * NOPE] = product(grad_scores, keys, 1, 0)
        rope_grad[:, head * ROPE : (head + 1) * ROPE] = product(grad_scores, shared, 1, 0)
        key_grads.append(product(grad_scores, nope, 0, 0))
        shared_grad = shared_grad + product(grad_scores, rope, 0, 0)
    stores = [
        pltpu.make_async_copy(nope_grad, nope_out, sems.at[0]),
        pltpu.make_async_copy(rope_grad, rope_out, sems.at[1]),
    ]
    for copy in stores:
        copy.start()
    key_grad = split(jnp.concatenate(key_grads, axis=1))
    value_grad = split(jnp.concatenate(value_grads, axis=1))

    latent_all[...] = product(key_grad, key_up, 1, 1) + product(value_grad, value_up, 1, 1)
    shared_all[...] = shared_grad
    for step in range(ways):
        at = rows_at(lax.rem(mine + step, ways), rows)
        pack_tokens(rows, lat, share_refs[step], latent_all[at, :], shared_all[at, :])

    up_grad[:, :width] = product(latent, key_grad, 0, 0)
    up_grad[:, width:] = product(latent, value_grad, 0, 0)
    for step in range(chips):
        keep_refs[step][...] = up_grad[rows_at(jnp.bitwise_xor(row, 2 * step), rows_up), :]
        send_ref[step, :, :] = up_grad[rows_at(jnp.bitwise_xor(row, 2 * step + 1), rows_up), :]
    for copy in stores:
        copy.wait()


def join_kernel(chips, *refs):
    received = refs[0]
    for step in range(chips):
        refs[1 + chips + step][...] = refs[1 + step][...] + received[step, :, :]


def token_sum_kernel(ways, *refs):
    latent_out, rope_out = refs[ways:]
    rows, lat = latent_out.shape
    total = refs[0][...]
    for step in range(1, ways):
        total = total + refs[step][...]
    latent_out[...] = total[:rows, :]
    rope_out[...] = unpack_narrow(rows, lat, total)


def up_sum_kernel(chips, *refs):
    key_out, value_out = refs[chips:]
    width = key_out.shape[1]
    total = refs[0][...]
    for step in range(1, chips):
        total = total + refs[step][...]
    key_out[...] = total[:, :width]
    value_out[...] = total[:, width:]


def vmem(*arrays):
    return [pltpu.with_memory_space_constraint(array, pltpu.VMEM) for array in arrays]


def stored(*arrays):
    return [pltpu.with_memory_space_constraint(array, pltpu.HBM) for array in arrays]


def hbm(*dims):
    return pltpu.HBM(dims, F32)


def limit(mebibytes):
    return pltpu.CompilerParams(vmem_limit_bytes=mebibytes << 20)


def on_device(fsdp, ways, query_nope, query_rope, latent, rope_key, cotangent, bounds, key_up, value_up):
    chips = fsdp // 2
    rows, lat = latent.shape
    rows_up, width = key_up.shape
    length = query_nope.shape[0]
    packed = rows + rows * ROPE // lat
    dma = pltpu.SemaphoreType.DMA

    def swap(x, step):
        return lax.ppermute(x, "fsdp", [(i, i ^ step) for i in range(fsdp)])

    def shift(x, step):
        return lax.ppermute(x, "head", [(i, (i + step) % ways) for i in range(ways)])

    tokens, ups = pl.pallas_call(
        pack_kernel, out_shape=(pltpu.VMEM((packed, lat), F32), pltpu.VMEM((2 * rows_up, width), F32)),
        in_specs=[HBM] * 4, out_specs=[VMEM] * 2,
        scratch_shapes=[pltpu.VMEM((rows, ROPE), F32), dma((4,))],
        compiler_params=limit(4), name="pack",
    )(*stored(latent, rope_key, key_up, value_up))
    token_blocks = [tokens] + [shift(tokens, step) for step in range(1, ways)]
    even = [ups] + [swap(ups, 2 * step) for step in range(1, chips)]
    odd = [swap(block, 1) for block in even]
    up_blocks = [block for pair in zip(even, odd) for block in pair]

    place = jnp.stack([lax.axis_index("head"), lax.axis_index("fsdp")]).astype(jnp.int32)
    out = pl.pallas_call(
        functools.partial(attention_kernel, ways, chips),
        out_shape=(
            hbm(length, width), hbm(*query_rope.shape), *([pltpu.VMEM((packed, lat), F32)] * ways),
            *([pltpu.VMEM((rows_up, 2 * width), F32)] * chips), pltpu.VMEM((chips, rows_up, 2 * width), F32),
        ),
        in_specs=[SMEM] * 2 + [VMEM] * (ways + fsdp) + [HBM] * 3,
        out_specs=[HBM] * 2 + [VMEM] * (ways + chips + 1),
        scratch_shapes=[
            pltpu.VMEM((length, lat), F32), pltpu.VMEM((length, ROPE), F32),
            pltpu.VMEM((lat, width), F32), pltpu.VMEM((lat, width), F32), pltpu.VMEM((lat, 2 * width), F32),
            pltpu.VMEM((length, width), F32), pltpu.VMEM(query_rope.shape, F32), pltpu.VMEM((length, width), F32),
            pltpu.VMEM((length, width), F32), pltpu.VMEM(query_rope.shape, F32), dma((3,)),
        ],
        compiler_params=limit(28), name="attention",
    )(place, bounds, *vmem(*token_blocks, *up_blocks), *stored(query_nope, query_rope, cotangent))
    nope_grad, rope_grad = out[:2]
    shares, keep, send = out[2 : 2 + ways], out[2 + ways : 2 + ways + chips], out[-1]

    received = swap(send, 1)
    joined = pl.pallas_call(
        functools.partial(join_kernel, chips), out_shape=[pltpu.VMEM((rows_up, 2 * width), F32)] * chips,
        in_specs=[VMEM] * (1 + chips), out_specs=[VMEM] * chips, compiler_params=limit(4), name="join",
    )(*vmem(received, *keep))
    arrived = [joined[0]] + [swap(joined[step], 2 * step) for step in range(1, chips)]
    pieces = [shares[0]] + [shift(shares[step], step) for step in range(1, ways)]
    latent_grad, rope_key_grad = pl.pallas_call(
        functools.partial(token_sum_kernel, ways), out_shape=(hbm(rows, lat), hbm(rows, ROPE)),
        in_specs=[VMEM] * ways, out_specs=[VMEM] * 2, compiler_params=limit(4), name="token_sum",
    )(*vmem(*pieces))
    key_up_grad, value_up_grad = pl.pallas_call(
        functools.partial(up_sum_kernel, chips), out_shape=(hbm(rows_up, width), hbm(rows_up, width)),
        in_specs=[VMEM] * chips, out_specs=[VMEM] * 2, compiler_params=limit(4), name="up_sum",
    )(*vmem(*arrived))
    return nope_grad, rope_grad, latent_grad, rope_key_grad, key_up_grad, value_up_grad


def solution(mesh):
    fsdp, ways = mesh.shape["fsdp"], mesh.shape["head"]

    def body(*args):
        return on_device(fsdp, ways, *args)

    return jax.shard_map(
        body,
        mesh=mesh,
        in_specs=(
            P("fsdp", "head"),
            P("fsdp", "head"),
            P(("fsdp", "head"), None),
            P(("fsdp", "head"), None),
            P("fsdp", "head"),
            P("fsdp", None),
            P("fsdp", "head"),
            P("fsdp", "head"),
        ),
        out_specs=(
            P("fsdp", "head"),
            P("fsdp", "head"),
            P(("fsdp", "head"), None),
            P(("fsdp", "head"), None),
            P("fsdp", "head"),
            P("fsdp", "head"),
        ),
        check_vma=False,
    )
```

```python
import functools

import jax
import jax.numpy as jnp
from jax import lax
from jax.experimental import pallas as pl
from jax.experimental.pallas import tpu as pltpu
from jax.sharding import PartitionSpec as P

NOPE = 128
ROPE = 64
VHEAD = 128
F32 = jnp.float32
BF16 = jnp.bfloat16


HBM = pl.BlockSpec(memory_space=pltpu.HBM)
VMEM = pl.BlockSpec(memory_space=pltpu.VMEM)
SMEM = pl.BlockSpec(memory_space=pltpu.SMEM)


def split(x):
    high = x.astype(BF16)
    return high, (x - high.astype(F32)).astype(BF16)


def product(left, right, left_dim, right_dim):
    dims = (((left_dim,), (right_dim,)), ((), ()))
    dot = functools.partial(lax.dot_general, dimension_numbers=dims, preferred_element_type=F32)
    return dot(left[0], right[0]) + (dot(left[0], right[1]) + dot(left[1], right[0]))


def columns(pair, start, size):
    return pair[0][:, start : start + size], pair[1][:, start : start + size]


def keep_pair(refs, x):
    pair = split(x)
    refs[0][...], refs[1][...] = pair
    return pair


def paired(ways):
    return ways & (ways - 1) == 0


def partner(mine, step, ways):
    return jnp.bitwise_xor(mine, step) if paired(ways) else lax.rem(mine + step, ways)


def rows_at(index, rows):
    return pl.ds(pl.multiple_of(index * rows, 8), rows)


def pack_tokens(rows, lat, out_ref, wide, narrow):
    folds = lat // ROPE
    fold = rows // folds
    out_ref[:rows, :] = wide
    for part in range(folds):
        out_ref[rows : rows + fold, part * ROPE : (part + 1) * ROPE] = narrow[part * fold : (part + 1) * fold, :]


def unpack_narrow(rows, lat, block):
    folds = lat // ROPE
    fold = rows // folds
    return jnp.concatenate([block[rows : rows + fold, part * ROPE : (part + 1) * ROPE] for part in range(folds)], axis=0)


def pack_kernel(latent_ref, rope_ref, key_ref, value_ref, tokens_out, ups_out, rope, sems):
    rows, lat = latent_ref.shape
    rows_up = key_ref.shape[0]
    copies = [
        pltpu.make_async_copy(rope_ref, rope, sems.at[0]),
        pltpu.make_async_copy(key_ref, ups_out.at[pl.ds(0, rows_up)], sems.at[1]),
        pltpu.make_async_copy(value_ref, ups_out.at[pl.ds(rows_up, rows_up)], sems.at[2]),
        pltpu.make_async_copy(latent_ref, tokens_out.at[pl.ds(0, rows)], sems.at[3]),
    ]
    for copy in copies:
        copy.start()
    copies[0].wait()
    folds = lat // ROPE
    fold = rows // folds
    for part in range(folds):
        tokens_out[rows : rows + fold, part * ROPE : (part + 1) * ROPE] = rope[part * fold : (part + 1) * fold, :]
    for copy in copies[1:]:
        copy.wait()


def prepare_kernel(limit_ref, nope_ref, rope_ref, cot_ref, mask_ref, *refs):
    factor = (NOPE + ROPE) ** (-0.5)
    query_pos = lax.broadcasted_iota(jnp.int32, mask_ref.shape, 0)
    key_pos = lax.broadcasted_iota(jnp.int32, mask_ref.shape, 1)
    visible = (key_pos < limit_ref[0, 1]) & ((key_pos <= query_pos) | (key_pos < limit_ref[0, 0]))
    mask_ref[...] = jnp.where(visible, 0.0, -jnp.inf)
    keep_pair(refs[0:2], nope_ref[...] * factor)
    keep_pair(refs[2:4], rope_ref[...] * factor)
    keep_pair(refs[4:6], cot_ref[...])


def attention_kernel(ways, chips, *refs):
    token_refs, refs = refs[:ways], refs[ways:]
    up_refs, refs = refs[: 2 * chips], refs[2 * chips :]
    mask_ref, nope_refs, rope_refs, cot_refs, refs = refs[0], refs[1:3], refs[3:5], refs[5:7], refs[7:]
    keep_refs, refs = refs[:chips], refs[chips:]
    send_ref, shared_grad_ref = refs[:2]
    grad_scores_refs, key_rows_refs, shared_refs = refs[2:4], refs[4:6], refs[6:8]
    key_grad_refs, value_grad_refs, key_up_refs, value_up_refs = refs[8:10], refs[10:12], refs[12:14], refs[14:16]
    latent_all, shared_all, key_all, value_all, up_grad = refs[16:]
    length, width = nope_refs[0].shape
    lat = latent_all.shape[1]
    rows = length // ways
    rows_up = up_refs[0].shape[0] // 2
    head_count = width // NOPE
    mine, row = lax.axis_index("head"), lax.axis_index("fsdp")

    for step in range(ways):
        at = rows_at(partner(mine, step, ways), rows)
        block = token_refs[step][...]
        latent_all[at, :] = block[:rows, :]
        shared_all[at, :] = unpack_narrow(rows, lat, block)
    for step in range(2 * chips):
        at = rows_at(jnp.bitwise_xor(row, step), rows_up)
        key_all[at, :] = up_refs[step][:rows_up, :]
        value_all[at, :] = up_refs[step][rows_up:, :]

    latent = split(latent_all[...])
    shared = keep_pair(shared_refs, shared_all[...])
    key_up = keep_pair(key_up_refs, key_all[...])
    value_up = keep_pair(value_up_refs, value_all[...])
    key_rows = keep_pair(key_rows_refs, product(latent, key_up, 1, 0))
    value_rows = split(product(latent, value_up, 1, 0))

    def of_head(refs, head, size):
        return refs[0][:, head * size : (head + 1) * size], refs[1][:, head * size : (head + 1) * size]

    def front(head):
        keys = columns(key_rows, head * NOPE, NOPE)
        values = columns(value_rows, head * VHEAD, VHEAD)
        scores = product(of_head(nope_refs, head, NOPE), keys, 1, 1)
        scores = scores + product(of_head(rope_refs, head, ROPE), shared, 1, 1)
        return scores + mask_ref[...], product(of_head(cot_refs, head, VHEAD), values, 1, 1)

    def middle(head, scores, grad_attend):
        weight = jnp.exp(scores - jnp.max(scores, axis=1, keepdims=True))
        attend = weight * (1.0 / jnp.sum(weight, axis=1, keepdims=True))
        weighted = attend * grad_attend
        grad_scores = keep_pair(
            [ref.at[head] for ref in grad_scores_refs],
            weighted - attend * jnp.sum(weighted, axis=1, keepdims=True),
        )
        return split(attend), grad_scores

    def back(head, attend, grad_scores):
        return (
            product(attend, of_head(cot_refs, head, VHEAD), 0, 0),
            product(grad_scores, of_head(nope_refs, head, NOPE), 0, 0),
            product(grad_scores, of_head(rope_refs, head, ROPE), 0, 0),
        )

    value_grads, key_grads = [], []
    shared_grad = jnp.zeros((length, ROPE), F32)
    ready = front(0)
    for head in range(head_count):
        later = front(head + 1) if head + 1 < head_count else None
        value_part, key_part, shared_part = back(head, *middle(head, *ready))
        value_grads.append(value_part)
        key_grads.append(key_part)
        shared_grad = shared_grad + shared_part
        ready = later
    shared_grad_ref[...] = shared_grad
    key_grad = keep_pair(key_grad_refs, jnp.concatenate(key_grads, axis=1))
    value_grad = keep_pair(value_grad_refs, jnp.concatenate(value_grads, axis=1))

    up_grad[:, :width] = product(latent, key_grad, 0, 0)
    up_grad[:, width:] = product(latent, value_grad, 0, 0)
    for step in range(chips):
        keep_refs[step][...] = up_grad[rows_at(jnp.bitwise_xor(row, 2 * step), rows_up), :]
        send_ref[step, :, :] = up_grad[rows_at(jnp.bitwise_xor(row, 2 * step + 1), rows_up), :]


def share_kernel(ways, shared_grad_ref, *refs):
    key_grad, value_grad, key_up, value_up = [
        (refs[2 * which][...], refs[2 * which + 1][...]) for which in range(4)
    ]
    share_refs, latent_all = refs[8 : 8 + ways], refs[8 + ways]
    rows = shared_grad_ref.shape[0] // ways
    lat = latent_all.shape[1]
    latent_all[...] = product(key_grad, key_up, 1, 1) + product(value_grad, value_up, 1, 1)
    for step in range(ways):
        at = rows_at(partner(lax.axis_index("head"), step, ways), rows)
        pack_tokens(rows, lat, share_refs[step], latent_all[at, :], shared_grad_ref[at, :])


def query_kernel(*refs):
    high_ref, low_ref = refs[:2]
    key_rows, shared = [(refs[2 * which][...], refs[2 * which + 1][...]) for which in (1, 2)]
    nope_out, rope_out = refs[6:]
    factor = (NOPE + ROPE) ** (-0.5)
    for head in range(high_ref.shape[0]):
        grad_scores = high_ref[head, :, :], low_ref[head, :, :]
        keys = columns(key_rows, head * NOPE, NOPE)
        nope_out[:, head * NOPE : (head + 1) * NOPE] = product(grad_scores, keys, 1, 0) * factor
        rope_out[:, head * ROPE : (head + 1) * ROPE] = product(grad_scores, shared, 1, 0) * factor


def join_kernel(chips, *refs):
    received = refs[0]
    for step in range(chips):
        refs[1 + chips + step][...] = refs[1 + step][...] + received[step, :, :]


def token_sum_kernel(ways, *refs):
    latent_out, rope_out = refs[ways:]
    rows, lat = latent_out.shape
    total = refs[0][...]
    for step in range(1, ways):
        total = total + refs[step][...]
    latent_out[...] = total[:rows, :]
    rope_out[...] = unpack_narrow(rows, lat, total)


def up_sum_kernel(chips, *refs):
    key_out, value_out = refs[chips:]
    width = key_out.shape[1]
    total = refs[0][...]
    for step in range(1, chips):
        total = total + refs[step][...]
    key_out[...] = total[:, :width]
    value_out[...] = total[:, width:]


def vmem(*arrays):
    return [pltpu.with_memory_space_constraint(array, pltpu.VMEM) for array in arrays]


def stored(*arrays):
    return [pltpu.with_memory_space_constraint(array, pltpu.HBM) for array in arrays]


def hbm(*dims):
    return pltpu.HBM(dims, F32)


def limit(mebibytes):
    return pltpu.CompilerParams(vmem_limit_bytes=mebibytes << 20)


def on_device(fsdp, ways, query_nope, query_rope, latent, rope_key, cotangent, bounds, key_up, value_up):
    chips = fsdp // 2
    rows, lat = latent.shape
    rows_up, width = key_up.shape
    length = query_nope.shape[0]
    packed = rows + rows * ROPE // lat
    dma = pltpu.SemaphoreType.DMA

    def swap(x, step):
        return lax.ppermute(x, "fsdp", [(i, i ^ step) for i in range(fsdp)])

    def shift(x, step):
        to = [(i, i ^ step if paired(ways) else (i + step) % ways) for i in range(ways)]
        return lax.ppermute(x, "head", to)

    tokens, ups = pl.pallas_call(
        pack_kernel, out_shape=(pltpu.VMEM((packed, lat), F32), pltpu.VMEM((2 * rows_up, width), F32)),
        in_specs=[HBM] * 4, out_specs=[VMEM] * 2,
        scratch_shapes=[pltpu.VMEM((rows, ROPE), F32), dma((4,))],
        compiler_params=limit(4), name="pack",
    )(*stored(latent, rope_key, key_up, value_up))
    token_blocks = [tokens] + [shift(tokens, step if paired(ways) else ways - step) for step in range(1, ways)]
    even = [ups] + [swap(ups, 2 * step) for step in range(1, chips)]
    odd = [swap(block, 1) for block in even]
    up_blocks = [block for pair in zip(even, odd) for block in pair]

    heads = width // NOPE
    wide, square = (length, width), (lat, width)
    pairs = [(heads, length, length), wide, (length, ROPE), wide, wide, square, square]
    queries = pl.pallas_call(
        prepare_kernel,
        out_shape=[pltpu.VMEM((length, length), F32)]
        + [pltpu.VMEM(dims, BF16) for dims in (wide, query_rope.shape, wide) for _ in range(2)],
        in_specs=[SMEM] + [VMEM] * 3, out_specs=[VMEM] * 7, compiler_params=limit(8), name="prepare",
    )(*stored(bounds, query_nope, query_rope, cotangent))
    out = pl.pallas_call(
        functools.partial(attention_kernel, ways, chips),
        out_shape=(
            *([pltpu.VMEM((rows_up, 2 * width), F32)] * chips), pltpu.VMEM((chips, rows_up, 2 * width), F32),
            pltpu.VMEM((length, ROPE), F32), *[pltpu.VMEM(dims, BF16) for dims in pairs for _ in range(2)],
        ),
        in_specs=[VMEM] * (ways + fsdp + 7),
        out_specs=[VMEM] * (chips + 2 + 2 * len(pairs)),
        scratch_shapes=[
            pltpu.VMEM((length, lat), F32), pltpu.VMEM((length, ROPE), F32),
            pltpu.VMEM(square, F32), pltpu.VMEM(square, F32), pltpu.VMEM((lat, 2 * width), F32),
        ],
        compiler_params=limit(24), name="attention",
    )(*vmem(*token_blocks, *up_blocks, *queries))
    keep, send, shared_grad, pairs = out[:chips], out[chips], out[chips + 1], out[chips + 2 :]

    shares = pl.pallas_call(
        functools.partial(share_kernel, ways), out_shape=[pltpu.VMEM((packed, lat), F32)] * ways,
        in_specs=[VMEM] * 9, out_specs=[VMEM] * ways,
        scratch_shapes=[pltpu.VMEM((length, lat), F32)], compiler_params=limit(8), name="share",
    )(*vmem(shared_grad, *pairs[6:]))
    nope_grad, rope_grad = pl.pallas_call(
        query_kernel, out_shape=(hbm(*wide), hbm(*query_rope.shape)),
        in_specs=[VMEM] * 6, out_specs=[VMEM] * 2, compiler_params=limit(8), name="query",
    )(*vmem(*pairs[:6]))

    received = swap(send, 1)
    joined = pl.pallas_call(
        functools.partial(join_kernel, chips), out_shape=[pltpu.VMEM((rows_up, 2 * width), F32)] * chips,
        in_specs=[VMEM] * (1 + chips), out_specs=[VMEM] * chips, compiler_params=limit(4), name="join",
    )(*vmem(received, *keep))
    arrived = [joined[0]] + [swap(joined[step], 2 * step) for step in range(1, chips)]
    pieces = [shares[0]] + [shift(shares[step], step) for step in range(1, ways)]
    latent_grad, rope_key_grad = pl.pallas_call(
        functools.partial(token_sum_kernel, ways), out_shape=(hbm(rows, lat), hbm(rows, ROPE)),
        in_specs=[VMEM] * ways, out_specs=[VMEM] * 2, compiler_params=limit(4), name="token_sum",
    )(*vmem(*pieces))
    key_up_grad, value_up_grad = pl.pallas_call(
        functools.partial(up_sum_kernel, chips), out_shape=(hbm(rows_up, width), hbm(rows_up, width)),
        in_specs=[VMEM] * chips, out_specs=[VMEM] * 2, compiler_params=limit(4), name="up_sum",
    )(*vmem(*arrived))
    return nope_grad, rope_grad, latent_grad, rope_key_grad, key_up_grad, value_up_grad


def solution(mesh):
    fsdp, ways = mesh.shape["fsdp"], mesh.shape["head"]

    def body(*args):
        return on_device(fsdp, ways, *args)

    return jax.shard_map(
        body,
        mesh=mesh,
        in_specs=(
            P("fsdp", "head"),
            P("fsdp", "head"),
            P(("fsdp", "head"), None),
            P(("fsdp", "head"), None),
            P("fsdp", "head"),
            P("fsdp", None),
            P("fsdp", "head"),
            P("fsdp", "head"),
        ),
        out_specs=(
            P("fsdp", "head"),
            P("fsdp", "head"),
            P(("fsdp", "head"), None),
            P(("fsdp", "head"), None),
            P("fsdp", "head"),
            P("fsdp", "head"),
        ),
        check_vma=False,
    )
```

```python
import functools

import jax
import jax.numpy as jnp
from jax import lax
from jax.experimental import pallas as pl
from jax.experimental.pallas import tpu as pltpu
from jax.sharding import PartitionSpec as P

NOPE = 128
ROPE = 64
VHEAD = 128
F32 = jnp.float32
BF16 = jnp.bfloat16


HBM = pl.BlockSpec(memory_space=pltpu.HBM)
VMEM = pl.BlockSpec(memory_space=pltpu.VMEM)
SMEM = pl.BlockSpec(memory_space=pltpu.SMEM)


def split(x):
    high = x.astype(BF16)
    return high, (x - high.astype(F32)).astype(BF16)


def product(left, right, left_dim, right_dim):
    dims = (((left_dim,), (right_dim,)), ((), ()))
    dot = functools.partial(lax.dot_general, dimension_numbers=dims, preferred_element_type=F32)
    return dot(left[0], right[0]) + (dot(left[0], right[1]) + dot(left[1], right[0]))


def columns(pair, start, size):
    return pair[0][:, start : start + size], pair[1][:, start : start + size]


def keep_pair(refs, x):
    pair = split(x)
    refs[0][...], refs[1][...] = pair
    return pair


def square(chips):
    return chips == 4


def paired(ways):
    return ways & (ways - 1) == 0


def partner(mine, step, ways):
    return jnp.bitwise_xor(mine, step) if paired(ways) else lax.rem(mine + step, ways)


def rows_at(index, rows):
    return pl.ds(pl.multiple_of(index * rows, 8), rows)


def pack_tokens(rows, lat, out_ref, wide, narrow):
    folds = lat // ROPE
    fold = rows // folds
    out_ref[:rows, :] = wide
    for part in range(folds):
        out_ref[rows : rows + fold, part * ROPE : (part + 1) * ROPE] = narrow[part * fold : (part + 1) * fold, :]


def unpack_narrow(rows, lat, block):
    folds = lat // ROPE
    fold = rows // folds
    return jnp.concatenate([block[rows : rows + fold, part * ROPE : (part + 1) * ROPE] for part in range(folds)], axis=0)


def pack_kernel(latent_ref, rope_ref, key_ref, value_ref, tokens_out, ups_out, rope, sems):
    rows, lat = latent_ref.shape
    rows_up = key_ref.shape[0]
    copies = [
        pltpu.make_async_copy(rope_ref, rope, sems.at[0]),
        pltpu.make_async_copy(key_ref, ups_out.at[pl.ds(0, rows_up)], sems.at[1]),
        pltpu.make_async_copy(value_ref, ups_out.at[pl.ds(rows_up, rows_up)], sems.at[2]),
        pltpu.make_async_copy(latent_ref, tokens_out.at[pl.ds(0, rows)], sems.at[3]),
    ]
    for copy in copies:
        copy.start()
    copies[0].wait()
    folds = lat // ROPE
    fold = rows // folds
    for part in range(folds):
        tokens_out[rows : rows + fold, part * ROPE : (part + 1) * ROPE] = rope[part * fold : (part + 1) * fold, :]
    for copy in copies[1:]:
        copy.wait()


def prepare_kernel(limit_ref, nope_ref, rope_ref, cot_ref, mask_ref, *refs):
    factor = (NOPE + ROPE) ** (-0.5)
    query_pos = lax.broadcasted_iota(jnp.int32, mask_ref.shape, 0)
    key_pos = lax.broadcasted_iota(jnp.int32, mask_ref.shape, 1)
    visible = (key_pos < limit_ref[0, 1]) & ((key_pos <= query_pos) | (key_pos < limit_ref[0, 0]))
    mask_ref[...] = jnp.where(visible, 0.0, -jnp.inf)
    keep_pair(refs[0:2], nope_ref[...] * factor)
    keep_pair(refs[2:4], rope_ref[...] * factor)
    keep_pair(refs[4:6], cot_ref[...])


def attention_kernel(ways, chips, *refs):
    token_refs, refs = refs[:ways], refs[ways:]
    up_refs, refs = refs[: 2 * chips], refs[2 * chips :]
    mask_ref, nope_refs, rope_refs, cot_refs, refs = refs[0], refs[1:3], refs[3:5], refs[5:7], refs[7:]
    keep_refs, refs = refs[:chips], refs[chips:]
    send_ref, shared_grad_ref = refs[:2]
    grad_scores_refs, key_rows_refs, shared_refs = refs[2:4], refs[4:6], refs[6:8]
    key_grad_refs, value_grad_refs, key_up_refs, value_up_refs = refs[8:10], refs[10:12], refs[12:14], refs[14:16]
    latent_all, shared_all, key_all, value_all, up_grad = refs[16:]
    length, width = nope_refs[0].shape
    lat = latent_all.shape[1]
    rows = length // ways
    rows_up = up_refs[0].shape[0] // 2
    head_count = width // NOPE
    mine, row = lax.axis_index("head"), lax.axis_index("fsdp")

    for step in range(ways):
        at = rows_at(partner(mine, step, ways), rows)
        block = token_refs[step][...]
        latent_all[at, :] = block[:rows, :]
        shared_all[at, :] = unpack_narrow(rows, lat, block)
    for step in range(2 * chips):
        at = rows_at(jnp.bitwise_xor(row, step), rows_up)
        key_all[at, :] = up_refs[step][:rows_up, :]
        value_all[at, :] = up_refs[step][rows_up:, :]

    latent = split(latent_all[...])
    shared = keep_pair(shared_refs, shared_all[...])
    key_up = keep_pair(key_up_refs, key_all[...])
    value_up = keep_pair(value_up_refs, value_all[...])
    key_rows = keep_pair(key_rows_refs, product(latent, key_up, 1, 0))
    value_rows = split(product(latent, value_up, 1, 0))

    def of_head(refs, head, size):
        return refs[0][:, head * size : (head + 1) * size], refs[1][:, head * size : (head + 1) * size]

    def front(head):
        keys = columns(key_rows, head * NOPE, NOPE)
        values = columns(value_rows, head * VHEAD, VHEAD)
        scores = product(of_head(nope_refs, head, NOPE), keys, 1, 1)
        scores = scores + product(of_head(rope_refs, head, ROPE), shared, 1, 1)
        return scores + mask_ref[...], product(of_head(cot_refs, head, VHEAD), values, 1, 1)

    def middle(head, scores, grad_attend):
        weight = jnp.exp(scores - jnp.max(scores, axis=1, keepdims=True))
        attend = weight * (1.0 / jnp.sum(weight, axis=1, keepdims=True))
        weighted = attend * grad_attend
        grad_scores = keep_pair(
            [ref.at[head] for ref in grad_scores_refs],
            weighted - attend * jnp.sum(weighted, axis=1, keepdims=True),
        )
        return split(attend), grad_scores

    def back(head, attend, grad_scores):
        return (
            product(attend, of_head(cot_refs, head, VHEAD), 0, 0),
            product(grad_scores, of_head(nope_refs, head, NOPE), 0, 0),
            product(grad_scores, of_head(rope_refs, head, ROPE), 0, 0),
        )

    value_grads, key_grads = [], []
    shared_grad = jnp.zeros((length, ROPE), F32)
    ready = front(0)
    for head in range(head_count):
        later = front(head + 1) if head + 1 < head_count else None
        value_part, key_part, shared_part = back(head, *middle(head, *ready))
        value_grads.append(value_part)
        key_grads.append(key_part)
        shared_grad = shared_grad + shared_part
        ready = later
    shared_grad_ref[...] = shared_grad
    key_grad = keep_pair(key_grad_refs, jnp.concatenate(key_grads, axis=1))
    value_grad = keep_pair(value_grad_refs, jnp.concatenate(value_grads, axis=1))

    up_grad[:, :width] = product(latent, key_grad, 0, 0)
    up_grad[:, width:] = product(latent, value_grad, 0, 0)
    for step in range(chips):
        keep_refs[step][...] = up_grad[rows_at(jnp.bitwise_xor(row, 2 * step), rows_up), :]
        send_ref[step, :, :] = up_grad[rows_at(jnp.bitwise_xor(row, 2 * step + 1), rows_up), :]


def share_kernel(ways, shared_grad_ref, *refs):
    key_grad, value_grad, key_up, value_up = [
        (refs[2 * which][...], refs[2 * which + 1][...]) for which in range(4)
    ]
    share_refs, latent_all = refs[8 : 8 + ways], refs[8 + ways]
    rows = shared_grad_ref.shape[0] // ways
    lat = latent_all.shape[1]
    latent_all[...] = product(key_grad, key_up, 1, 1) + product(value_grad, value_up, 1, 1)
    for step in range(ways):
        at = rows_at(partner(lax.axis_index("head"), step, ways), rows)
        pack_tokens(rows, lat, share_refs[step], latent_all[at, :], shared_grad_ref[at, :])


def query_kernel(*refs):
    high_ref, low_ref = refs[:2]
    key_rows, shared = [(refs[2 * which][...], refs[2 * which + 1][...]) for which in (1, 2)]
    nope_out, rope_out = refs[6:]
    factor = (NOPE + ROPE) ** (-0.5)
    for head in range(high_ref.shape[0]):
        grad_scores = high_ref[head, :, :], low_ref[head, :, :]
        keys = columns(key_rows, head * NOPE, NOPE)
        nope_out[:, head * NOPE : (head + 1) * NOPE] = product(grad_scores, keys, 1, 0) * factor
        rope_out[:, head * ROPE : (head + 1) * ROPE] = product(grad_scores, shared, 1, 0) * factor


def join_kernel(chips, *refs):
    received, keep, outs = refs[0], refs[1 : 1 + chips], refs[1 + chips :]
    width = outs[0].shape[1]
    for step in range(chips):
        total = keep[step][...] + received[step, :, :]
        outs[step][...] = total[:, :width]
        outs[chips + step][...] = total[:, width:]


def add_kernel(*refs):
    count = len(refs) // 3
    for which in range(count):
        refs[2 * count + which][...] = refs[which][...] + refs[count + which][...]


def token_sum_kernel(ways, *refs):
    latent_out, rope_out = refs[ways:]
    rows, lat = latent_out.shape
    total = refs[0][...]
    for step in range(1, ways):
        total = total + refs[step][...]
    latent_out[...] = total[:rows, :]
    rope_out[...] = unpack_narrow(rows, lat, total)


def up_sum_kernel(*refs):
    count = len(refs) // 2 - 1
    for out, parts in ((refs[-2], refs[:count]), (refs[-1], refs[count:-2])):
        total = parts[0][...]
        for part in parts[1:]:
            total = total + part[...]
        out[...] = total


def vmem(*arrays):
    return [pltpu.with_memory_space_constraint(array, pltpu.VMEM) for array in arrays]


def stored(*arrays):
    return [pltpu.with_memory_space_constraint(array, pltpu.HBM) for array in arrays]


def hbm(*dims):
    return pltpu.HBM(dims, F32)


def limit(mebibytes):
    return pltpu.CompilerParams(vmem_limit_bytes=mebibytes << 20)


def on_device(fsdp, ways, query_nope, query_rope, latent, rope_key, cotangent, bounds, key_up, value_up):
    chips = fsdp // 2
    rows, lat = latent.shape
    rows_up, width = key_up.shape
    length = query_nope.shape[0]
    packed = rows + rows * ROPE // lat
    dma = pltpu.SemaphoreType.DMA

    def swap(x, step):
        return lax.ppermute(x, "fsdp", [(i, i ^ step) for i in range(fsdp)])

    def shift(x, step):
        to = [(i, i ^ step if paired(ways) else (i + step) % ways) for i in range(ways)]
        return lax.ppermute(x, "head", to)

    tokens, ups = pl.pallas_call(
        pack_kernel, out_shape=(pltpu.VMEM((packed, lat), F32), pltpu.VMEM((2 * rows_up, width), F32)),
        in_specs=[HBM] * 4, out_specs=[VMEM] * 2,
        scratch_shapes=[pltpu.VMEM((rows, ROPE), F32), dma((4,))],
        compiler_params=limit(4), name="pack",
    )(*stored(latent, rope_key, key_up, value_up))
    token_blocks = [tokens] + [shift(tokens, step if paired(ways) else ways - step) for step in range(1, ways)]
    even = [ups] + [swap(ups, 2 * step) for step in range(1, chips)]
    odd = [swap(block, 1) for block in even]
    up_blocks = [block for pair in zip(even, odd) for block in pair]

    heads = width // NOPE
    wide, whole = (length, width), (lat, width)
    pairs = [(heads, length, length), wide, (length, ROPE), wide, wide, whole, whole]
    queries = pl.pallas_call(
        prepare_kernel,
        out_shape=[pltpu.VMEM((length, length), F32)]
        + [pltpu.VMEM(dims, BF16) for dims in (wide, query_rope.shape, wide) for _ in range(2)],
        in_specs=[SMEM] + [VMEM] * 3, out_specs=[VMEM] * 7, compiler_params=limit(8), name="prepare",
    )(*stored(bounds, query_nope, query_rope, cotangent))
    out = pl.pallas_call(
        functools.partial(attention_kernel, ways, chips),
        out_shape=(
            *([pltpu.VMEM((rows_up, 2 * width), F32)] * chips), pltpu.VMEM((chips, rows_up, 2 * width), F32),
            pltpu.VMEM((length, ROPE), F32), *[pltpu.VMEM(dims, BF16) for dims in pairs for _ in range(2)],
        ),
        in_specs=[VMEM] * (ways + fsdp + 7),
        out_specs=[VMEM] * (chips + 2 + 2 * len(pairs)),
        scratch_shapes=[
            pltpu.VMEM((length, lat), F32), pltpu.VMEM((length, ROPE), F32),
            pltpu.VMEM(whole, F32), pltpu.VMEM(whole, F32), pltpu.VMEM((lat, 2 * width), F32),
        ],
        compiler_params=limit(24), name="attention",
    )(*vmem(*token_blocks, *up_blocks, *queries))
    keep, send, shared_grad, pairs = out[:chips], out[chips], out[chips + 1], out[chips + 2 :]

    shares = pl.pallas_call(
        functools.partial(share_kernel, ways), out_shape=[pltpu.VMEM((packed, lat), F32)] * ways,
        in_specs=[VMEM] * 9, out_specs=[VMEM] * ways,
        scratch_shapes=[pltpu.VMEM((length, lat), F32)], compiler_params=limit(8), name="share",
    )(*vmem(shared_grad, *pairs[6:]))
    nope_grad, rope_grad = pl.pallas_call(
        query_kernel, out_shape=(hbm(*wide), hbm(*query_rope.shape)),
        in_specs=[VMEM] * 6, out_specs=[VMEM] * 2, compiler_params=limit(8), name="query",
    )(*vmem(*pairs[:6]))

    block = pltpu.VMEM((rows_up, width), F32)
    received = swap(send, 1)
    joined = pl.pallas_call(
        functools.partial(join_kernel, chips), out_shape=[block] * (2 * chips),
        in_specs=[VMEM] * (1 + chips), out_specs=[VMEM] * (2 * chips), compiler_params=limit(6), name="join",
    )(*vmem(received, *keep))
    keys, values = list(joined[:chips]), list(joined[chips:])
    if square(chips):
        relayed = swap(keys[3], 2), swap(values[3], 4)
        direct = swap(keys[1], 2), swap(values[2], 4)
        added = pl.pallas_call(
            add_kernel, out_shape=[block] * 2, in_specs=[VMEM] * 4, out_specs=[VMEM] * 2,
            compiler_params=limit(4), name="relay",
        )(*vmem(keys[2], values[1], *relayed))
        key_parts = [keys[0], direct[0], swap(added[0], 4)]
        value_parts = [values[0], direct[1], swap(added[1], 2)]
    else:
        key_parts = keys[:1] + [swap(keys[step], 2 * step) for step in range(1, chips)]
        value_parts = values[:1] + [swap(values[step], 2 * step) for step in range(1, chips)]
    pieces = [shares[0]] + [shift(shares[step], step) for step in range(1, ways)]
    latent_grad, rope_key_grad = pl.pallas_call(
        functools.partial(token_sum_kernel, ways), out_shape=(hbm(rows, lat), hbm(rows, ROPE)),
        in_specs=[VMEM] * ways, out_specs=[VMEM] * 2, compiler_params=limit(4), name="token_sum",
    )(*vmem(*pieces))
    key_up_grad, value_up_grad = pl.pallas_call(
        up_sum_kernel, out_shape=(hbm(rows_up, width), hbm(rows_up, width)),
        in_specs=[VMEM] * (2 * len(key_parts)), out_specs=[VMEM] * 2, compiler_params=limit(4), name="up_sum",
    )(*vmem(*key_parts, *value_parts))
    return nope_grad, rope_grad, latent_grad, rope_key_grad, key_up_grad, value_up_grad


def solution(mesh):
    fsdp, ways = mesh.shape["fsdp"], mesh.shape["head"]

    def body(*args):
        return on_device(fsdp, ways, *args)

    return jax.shard_map(
        body,
        mesh=mesh,
        in_specs=(
            P("fsdp", "head"),
            P("fsdp", "head"),
            P(("fsdp", "head"), None),
            P(("fsdp", "head"), None),
            P("fsdp", "head"),
            P("fsdp", None),
            P("fsdp", "head"),
            P("fsdp", "head"),
        ),
        out_specs=(
            P("fsdp", "head"),
            P("fsdp", "head"),
            P(("fsdp", "head"), None),
            P(("fsdp", "head"), None),
            P("fsdp", "head"),
            P("fsdp", "head"),
        ),
        check_vma=False,
    )
```

```python
import functools

import jax
import jax.numpy as jnp
from jax import lax
from jax.experimental import pallas as pl
from jax.experimental.pallas import tpu as pltpu
from jax.sharding import PartitionSpec as P

NOPE = 128
ROPE = 64
VHEAD = 128
F32 = jnp.float32
BF16 = jnp.bfloat16


HBM = pl.BlockSpec(memory_space=pltpu.HBM)
VMEM = pl.BlockSpec(memory_space=pltpu.VMEM)
SMEM = pl.BlockSpec(memory_space=pltpu.SMEM)


def split(x):
    high = x.astype(BF16)
    return high, (x - high.astype(F32)).astype(BF16)


def product(left, right, left_dim, right_dim):
    dims = (((left_dim,), (right_dim,)), ((), ()))
    dot = functools.partial(lax.dot_general, dimension_numbers=dims, preferred_element_type=F32)
    return dot(left[0], right[0]) + (dot(left[0], right[1]) + dot(left[1], right[0]))


def joined_dot(left, right):
    left, right = jnp.concatenate(left, axis=1), jnp.concatenate(right, axis=1)
    return lax.dot_general(left, right, (((1,), (1,)), ((), ())), preferred_element_type=F32)


def over_rows(left, right):
    return lax.dot_general(left, right, (((0,), (0,)), ((), ())), preferred_element_type=F32)


def columns(pair, start, size):
    return pair[0][:, start : start + size], pair[1][:, start : start + size]


def keep_pair(refs, x):
    pair = split(x)
    refs[0][...], refs[1][...] = pair
    return pair


def square(chips):
    return chips == 4


def paired(ways):
    return ways & (ways - 1) == 0


def partner(mine, step, ways):
    return jnp.bitwise_xor(mine, step) if paired(ways) else lax.rem(mine + step, ways)


def rows_at(index, rows):
    return pl.ds(pl.multiple_of(index * rows, 8), rows)


def pack_tokens(rows, lat, out_ref, wide, narrow):
    folds = lat // ROPE
    fold = rows // folds
    out_ref[:rows, :] = wide
    for part in range(folds):
        out_ref[rows : rows + fold, part * ROPE : (part + 1) * ROPE] = narrow[part * fold : (part + 1) * fold, :]


def unpack_narrow(rows, lat, block):
    folds = lat // ROPE
    fold = rows // folds
    return jnp.concatenate([block[rows : rows + fold, part * ROPE : (part + 1) * ROPE] for part in range(folds)], axis=0)


def pack_kernel(latent_ref, rope_ref, key_ref, value_ref, tokens_out, ups_out, rope, sems):
    rows, lat = latent_ref.shape
    rows_up = key_ref.shape[0]
    copies = [
        pltpu.make_async_copy(rope_ref, rope, sems.at[0]),
        pltpu.make_async_copy(key_ref, ups_out.at[pl.ds(0, rows_up)], sems.at[1]),
        pltpu.make_async_copy(value_ref, ups_out.at[pl.ds(rows_up, rows_up)], sems.at[2]),
        pltpu.make_async_copy(latent_ref, tokens_out.at[pl.ds(0, rows)], sems.at[3]),
    ]
    for copy in copies:
        copy.start()
    copies[0].wait()
    folds = lat // ROPE
    fold = rows // folds
    for part in range(folds):
        tokens_out[rows : rows + fold, part * ROPE : (part + 1) * ROPE] = rope[part * fold : (part + 1) * fold, :]
    for copy in copies[1:]:
        copy.wait()


def prepare_kernel(limit_ref, nope_ref, rope_ref, cot_ref, mask_ref, *refs):
    factor = (NOPE + ROPE) ** (-0.5)
    query_pos = lax.broadcasted_iota(jnp.int32, mask_ref.shape, 0)
    key_pos = lax.broadcasted_iota(jnp.int32, mask_ref.shape, 1)
    visible = (key_pos < limit_ref[0, 1]) & ((key_pos <= query_pos) | (key_pos < limit_ref[0, 0]))
    mask_ref[...] = jnp.where(visible, 0.0, -jnp.inf)
    rope_ref_out, nope_refs, cot_refs = refs[0], refs[1:3], refs[3:5]
    keep_pair(nope_refs, nope_ref[...] * factor)
    keep_pair(cot_refs, cot_ref[...])
    rope = split(rope_ref[...] * factor)
    for head in range(rope_ref_out.shape[0]):
        high, low = columns(rope, head * ROPE, ROPE)
        rope_ref_out[head, :, :] = jnp.concatenate([high, low, high], axis=1)


def attention_kernel(ways, chips, *refs):
    token_refs, refs = refs[:ways], refs[ways:]
    up_refs, refs = refs[: 2 * chips], refs[2 * chips :]
    mask_ref, rope_ref, nope_refs, cot_refs, refs = refs[0], refs[1], refs[2:4], refs[4:6], refs[6:]
    keep_refs, refs = refs[:chips], refs[chips:]
    send_ref, shared_grad_ref = refs[:2]
    grad_scores_refs, key_rows_refs, shared_refs = refs[2:4], refs[4:6], refs[6:8]
    key_grad_refs, value_grad_refs, key_up_refs, value_up_refs = refs[8:10], refs[10:12], refs[12:14], refs[14:16]
    latent_all, shared_all, key_all, value_all, up_grad = refs[16:]
    length, width = nope_refs[0].shape
    lat = latent_all.shape[1]
    rows = length // ways
    rows_up = up_refs[0].shape[0] // 2
    head_count = width // NOPE
    mine, row = lax.axis_index("head"), lax.axis_index("fsdp")

    for step in range(ways):
        at = rows_at(partner(mine, step, ways), rows)
        block = token_refs[step][...]
        latent_all[at, :] = block[:rows, :]
        shared_all[at, :] = unpack_narrow(rows, lat, block)
    for step in range(2 * chips):
        at = rows_at(jnp.bitwise_xor(row, step), rows_up)
        key_all[at, :] = up_refs[step][:rows_up, :]
        value_all[at, :] = up_refs[step][rows_up:, :]

    latent = split(latent_all[...])
    shared = keep_pair(shared_refs, shared_all[...])
    key_up = keep_pair(key_up_refs, key_all[...])
    value_up = keep_pair(value_up_refs, value_all[...])
    key_rows = keep_pair(key_rows_refs, product(latent, key_up, 1, 0))
    value_rows = split(product(latent, value_up, 1, 0))

    shared_parts = jnp.concatenate([shared[0], shared[0], shared[1]], axis=1)

    def front(head):
        nope, cot = columns(nope_refs, head * NOPE, NOPE), columns(cot_refs, head * VHEAD, VHEAD)
        keys, values = columns(key_rows, head * NOPE, NOPE), columns(value_rows, head * VHEAD, VHEAD)
        scores = joined_dot([*nope, nope[0], rope_ref[head]], [keys[0], *keys, shared_parts])
        return scores + mask_ref[...], joined_dot([*cot, cot[0]], [values[0], *values])

    def middle(head, scores, grad_attend):
        weight = jnp.exp(scores - jnp.max(scores, axis=1, keepdims=True))
        attend = weight * (1.0 / jnp.sum(weight, axis=1, keepdims=True))
        weighted = attend * grad_attend
        grad_scores = keep_pair(
            [ref.at[head] for ref in grad_scores_refs],
            weighted - attend * jnp.sum(weighted, axis=1, keepdims=True),
        )
        return split(attend), grad_scores

    def back(head, attend, grad_scores):
        nope, cot = columns(nope_refs, head * NOPE, NOPE), columns(cot_refs, head * VHEAD, VHEAD)
        rope = rope_ref[head][:, : 2 * ROPE]
        both_cot = over_rows(attend[0], jnp.concatenate(cot, axis=1))
        both_nope = over_rows(grad_scores[0], jnp.concatenate(nope, axis=1))
        low = over_rows(grad_scores[1], jnp.concatenate([nope[0], rope], axis=1))
        return (
            both_cot[:, :VHEAD] + both_cot[:, VHEAD:] + over_rows(attend[1], cot[0]),
            both_nope[:, :NOPE] + both_nope[:, NOPE:] + low[:, :NOPE],
            over_rows(grad_scores[0], rope) + low[:, NOPE:],
        )

    value_grads, key_grads = [], []
    shared_grad = jnp.zeros((length, 2 * ROPE), F32)
    ready = front(0)
    for head in range(head_count):
        later = front(head + 1) if head + 1 < head_count else None
        value_part, key_part, shared_part = back(head, *middle(head, *ready))
        value_grads.append(value_part)
        key_grads.append(key_part)
        shared_grad = shared_grad + shared_part
        ready = later
    shared_grad_ref[...] = shared_grad[:, :ROPE] + shared_grad[:, ROPE:]
    key_grad = keep_pair(key_grad_refs, jnp.concatenate(key_grads, axis=1))
    value_grad = keep_pair(value_grad_refs, jnp.concatenate(value_grads, axis=1))

    up_grad[:, :width] = product(latent, key_grad, 0, 0)
    up_grad[:, width:] = product(latent, value_grad, 0, 0)
    for step in range(chips):
        keep_refs[step][...] = up_grad[rows_at(jnp.bitwise_xor(row, 2 * step), rows_up), :]
        send_ref[step, :, :] = up_grad[rows_at(jnp.bitwise_xor(row, 2 * step + 1), rows_up), :]


def share_kernel(ways, shared_grad_ref, *refs):
    key_grad, value_grad, key_up, value_up = [
        (refs[2 * which][...], refs[2 * which + 1][...]) for which in range(4)
    ]
    share_refs, latent_all = refs[8 : 8 + ways], refs[8 + ways]
    rows = shared_grad_ref.shape[0] // ways
    lat = latent_all.shape[1]
    latent_all[...] = product(key_grad, key_up, 1, 1) + product(value_grad, value_up, 1, 1)
    for step in range(ways):
        at = rows_at(partner(lax.axis_index("head"), step, ways), rows)
        pack_tokens(rows, lat, share_refs[step], latent_all[at, :], shared_grad_ref[at, :])


def query_kernel(*refs):
    high_ref, low_ref = refs[:2]
    key_rows, shared = [(refs[2 * which][...], refs[2 * which + 1][...]) for which in (1, 2)]
    nope_out, rope_out = refs[6:]
    factor = (NOPE + ROPE) ** (-0.5)
    for head in range(high_ref.shape[0]):
        grad_scores = high_ref[head, :, :], low_ref[head, :, :]
        keys = columns(key_rows, head * NOPE, NOPE)
        nope_out[:, head * NOPE : (head + 1) * NOPE] = product(grad_scores, keys, 1, 0) * factor
        rope_out[:, head * ROPE : (head + 1) * ROPE] = product(grad_scores, shared, 1, 0) * factor


def join_kernel(chips, *refs):
    received, keep, outs = refs[0], refs[1 : 1 + chips], refs[1 + chips :]
    width = outs[0].shape[1]
    for step in range(chips):
        total = keep[step][...] + received[step, :, :]
        outs[step][...] = total[:, :width]
        outs[chips + step][...] = total[:, width:]


def add_kernel(*refs):
    count = len(refs) // 3
    for which in range(count):
        refs[2 * count + which][...] = refs[which][...] + refs[count + which][...]


def token_sum_kernel(ways, *refs):
    latent_out, rope_out = refs[ways:]
    rows, lat = latent_out.shape
    total = refs[0][...]
    for step in range(1, ways):
        total = total + refs[step][...]
    latent_out[...] = total[:rows, :]
    rope_out[...] = unpack_narrow(rows, lat, total)


def up_sum_kernel(*refs):
    count = len(refs) // 2 - 1
    for out, parts in ((refs[-2], refs[:count]), (refs[-1], refs[count:-2])):
        total = parts[0][...]
        for part in parts[1:]:
            total = total + part[...]
        out[...] = total


def vmem(*arrays):
    return [pltpu.with_memory_space_constraint(array, pltpu.VMEM) for array in arrays]


def stored(*arrays):
    return [pltpu.with_memory_space_constraint(array, pltpu.HBM) for array in arrays]


def hbm(*dims):
    return pltpu.HBM(dims, F32)


def limit(mebibytes):
    return pltpu.CompilerParams(vmem_limit_bytes=mebibytes << 20)


def on_device(fsdp, ways, query_nope, query_rope, latent, rope_key, cotangent, bounds, key_up, value_up):
    chips = fsdp // 2
    rows, lat = latent.shape
    rows_up, width = key_up.shape
    length = query_nope.shape[0]
    packed = rows + rows * ROPE // lat
    dma = pltpu.SemaphoreType.DMA

    def swap(x, step):
        return lax.ppermute(x, "fsdp", [(i, i ^ step) for i in range(fsdp)])

    def shift(x, step):
        to = [(i, i ^ step if paired(ways) else (i + step) % ways) for i in range(ways)]
        return lax.ppermute(x, "head", to)

    tokens, ups = pl.pallas_call(
        pack_kernel, out_shape=(pltpu.VMEM((packed, lat), F32), pltpu.VMEM((2 * rows_up, width), F32)),
        in_specs=[HBM] * 4, out_specs=[VMEM] * 2,
        scratch_shapes=[pltpu.VMEM((rows, ROPE), F32), dma((4,))],
        compiler_params=limit(4), name="pack",
    )(*stored(latent, rope_key, key_up, value_up))
    token_blocks = [tokens] + [shift(tokens, step if paired(ways) else ways - step) for step in range(1, ways)]
    even = [ups] + [swap(ups, 2 * step) for step in range(1, chips)]
    odd = [swap(block, 1) for block in even]
    up_blocks = [block for pair in zip(even, odd) for block in pair]

    heads = width // NOPE
    wide, whole = (length, width), (lat, width)
    pairs = [(heads, length, length), wide, (length, ROPE), wide, wide, whole, whole]
    queries = pl.pallas_call(
        prepare_kernel,
        out_shape=[pltpu.VMEM((length, length), F32)]
        + [pltpu.VMEM((heads, length, 3 * ROPE), BF16)] + [pltpu.VMEM(wide, BF16)] * 4,
        in_specs=[SMEM] + [VMEM] * 3, out_specs=[VMEM] * 6, compiler_params=limit(8), name="prepare",
    )(*stored(bounds, query_nope, query_rope, cotangent))
    out = pl.pallas_call(
        functools.partial(attention_kernel, ways, chips),
        out_shape=(
            *([pltpu.VMEM((rows_up, 2 * width), F32)] * chips), pltpu.VMEM((chips, rows_up, 2 * width), F32),
            pltpu.VMEM((length, ROPE), F32), *[pltpu.VMEM(dims, BF16) for dims in pairs for _ in range(2)],
        ),
        in_specs=[VMEM] * (ways + fsdp + 6),
        out_specs=[VMEM] * (chips + 2 + 2 * len(pairs)),
        scratch_shapes=[
            pltpu.VMEM((length, lat), F32), pltpu.VMEM((length, ROPE), F32),
            pltpu.VMEM(whole, F32), pltpu.VMEM(whole, F32), pltpu.VMEM((lat, 2 * width), F32),
        ],
        compiler_params=limit(24), name="attention",
    )(*vmem(*token_blocks, *up_blocks, *queries))
    keep, send, shared_grad, pairs = out[:chips], out[chips], out[chips + 1], out[chips + 2 :]

    shares = pl.pallas_call(
        functools.partial(share_kernel, ways), out_shape=[pltpu.VMEM((packed, lat), F32)] * ways,
        in_specs=[VMEM] * 9, out_specs=[VMEM] * ways,
        scratch_shapes=[pltpu.VMEM((length, lat), F32)], compiler_params=limit(8), name="share",
    )(*vmem(shared_grad, *pairs[6:]))
    nope_grad, rope_grad = pl.pallas_call(
        query_kernel, out_shape=(hbm(*wide), hbm(*query_rope.shape)),
        in_specs=[VMEM] * 6, out_specs=[VMEM] * 2, compiler_params=limit(8), name="query",
    )(*vmem(*pairs[:6]))

    block = pltpu.VMEM((rows_up, width), F32)
    received = swap(send, 1)
    joined = pl.pallas_call(
        functools.partial(join_kernel, chips), out_shape=[block] * (2 * chips),
        in_specs=[VMEM] * (1 + chips), out_specs=[VMEM] * (2 * chips), compiler_params=limit(6), name="join",
    )(*vmem(received, *keep))
    keys, values = list(joined[:chips]), list(joined[chips:])
    if square(chips):
        relayed = swap(keys[3], 2), swap(values[3], 4)
        direct = swap(keys[1], 2), swap(values[2], 4)
        added = pl.pallas_call(
            add_kernel, out_shape=[block] * 2, in_specs=[VMEM] * 4, out_specs=[VMEM] * 2,
            compiler_params=limit(4), name="relay",
        )(*vmem(keys[2], values[1], *relayed))
        key_parts = [keys[0], direct[0], swap(added[0], 4)]
        value_parts = [values[0], direct[1], swap(added[1], 2)]
    else:
        key_parts = keys[:1] + [swap(keys[step], 2 * step) for step in range(1, chips)]
        value_parts = values[:1] + [swap(values[step], 2 * step) for step in range(1, chips)]
    pieces = [shares[0]] + [shift(shares[step], step) for step in range(1, ways)]
    latent_grad, rope_key_grad = pl.pallas_call(
        functools.partial(token_sum_kernel, ways), out_shape=(hbm(rows, lat), hbm(rows, ROPE)),
        in_specs=[VMEM] * ways, out_specs=[VMEM] * 2, compiler_params=limit(4), name="token_sum",
    )(*vmem(*pieces))
    key_up_grad, value_up_grad = pl.pallas_call(
        up_sum_kernel, out_shape=(hbm(rows_up, width), hbm(rows_up, width)),
        in_specs=[VMEM] * (2 * len(key_parts)), out_specs=[VMEM] * 2, compiler_params=limit(4), name="up_sum",
    )(*vmem(*key_parts, *value_parts))
    return nope_grad, rope_grad, latent_grad, rope_key_grad, key_up_grad, value_up_grad


def solution(mesh):
    fsdp, ways = mesh.shape["fsdp"], mesh.shape["head"]

    def body(*args):
        return on_device(fsdp, ways, *args)

    return jax.shard_map(
        body,
        mesh=mesh,
        in_specs=(
            P("fsdp", "head"),
            P("fsdp", "head"),
            P(("fsdp", "head"), None),
            P(("fsdp", "head"), None),
            P("fsdp", "head"),
            P("fsdp", None),
            P("fsdp", "head"),
            P("fsdp", "head"),
        ),
        out_specs=(
            P("fsdp", "head"),
            P("fsdp", "head"),
            P(("fsdp", "head"), None),
            P(("fsdp", "head"), None),
            P("fsdp", "head"),
            P("fsdp", "head"),
        ),
        check_vma=False,
    )
```

```python
import functools

import jax
import jax.numpy as jnp
from jax import lax
from jax.experimental import pallas as pl
from jax.experimental.pallas import tpu as pltpu
from jax.sharding import PartitionSpec as P

NOPE = 128
ROPE = 64
VHEAD = 128
F32 = jnp.float32
BF16 = jnp.bfloat16


HBM = pl.BlockSpec(memory_space=pltpu.HBM)
VMEM = pl.BlockSpec(memory_space=pltpu.VMEM)
SMEM = pl.BlockSpec(memory_space=pltpu.SMEM)


def split(x):
    high = x.astype(BF16)
    return high, (x - high.astype(F32)).astype(BF16)


def product(left, right, left_dim, right_dim):
    dims = (((left_dim,), (right_dim,)), ((), ()))
    dot = functools.partial(lax.dot_general, dimension_numbers=dims, preferred_element_type=F32)
    return dot(left[0], right[0]) + (dot(left[0], right[1]) + dot(left[1], right[0]))


def joined_dot(left, right):
    left, right = jnp.concatenate(left, axis=1), jnp.concatenate(right, axis=1)
    return lax.dot_general(left, right, (((1,), (1,)), ((), ())), preferred_element_type=F32)


def over_rows(left, right):
    return lax.dot_general(left, right, (((0,), (0,)), ((), ())), preferred_element_type=F32)


def columns(pair, start, size):
    return pair[0][:, start : start + size], pair[1][:, start : start + size]


def keep_pair(refs, x):
    pair = split(x)
    refs[0][...], refs[1][...] = pair
    return pair


def square(chips):
    return chips == 4


def partner(mine, step, ways):
    return lax.rem(mine + step, ways)


def rows_at(index, rows):
    return pl.ds(pl.multiple_of(index * rows, 8), rows)


def pack_tokens(rows, lat, out_ref, wide, narrow):
    folds = lat // ROPE
    fold = rows // folds
    out_ref[:rows, :] = wide
    for part in range(folds):
        out_ref[rows : rows + fold, part * ROPE : (part + 1) * ROPE] = narrow[part * fold : (part + 1) * fold, :]


def unpack_narrow(rows, lat, block):
    folds = lat // ROPE
    fold = rows // folds
    return jnp.concatenate([block[rows : rows + fold, part * ROPE : (part + 1) * ROPE] for part in range(folds)], axis=0)


def pack_kernel(latent_ref, rope_ref, key_ref, value_ref, tokens_out, ups_out, rope, sems):
    rows, lat = latent_ref.shape
    rows_up = key_ref.shape[0]
    copies = [
        pltpu.make_async_copy(rope_ref, rope, sems.at[0]),
        pltpu.make_async_copy(key_ref, ups_out.at[pl.ds(0, rows_up)], sems.at[1]),
        pltpu.make_async_copy(value_ref, ups_out.at[pl.ds(rows_up, rows_up)], sems.at[2]),
        pltpu.make_async_copy(latent_ref, tokens_out.at[pl.ds(0, rows)], sems.at[3]),
    ]
    for copy in copies:
        copy.start()
    copies[0].wait()
    folds = lat // ROPE
    fold = rows // folds
    for part in range(folds):
        tokens_out[rows : rows + fold, part * ROPE : (part + 1) * ROPE] = rope[part * fold : (part + 1) * fold, :]
    for copy in copies[1:]:
        copy.wait()


def prepare_kernel(limit_ref, nope_ref, rope_ref, cot_ref, mask_ref, *refs):
    factor = (NOPE + ROPE) ** (-0.5)
    query_pos = lax.broadcasted_iota(jnp.int32, mask_ref.shape, 0)
    key_pos = lax.broadcasted_iota(jnp.int32, mask_ref.shape, 1)
    visible = (key_pos < limit_ref[0, 1]) & ((key_pos <= query_pos) | (key_pos < limit_ref[0, 0]))
    mask_ref[...] = jnp.where(visible, 0.0, -jnp.inf)
    rope_ref_out, nope_refs, cot_refs = refs[0], refs[1:3], refs[3:5]
    keep_pair(nope_refs, nope_ref[...] * factor)
    keep_pair(cot_refs, cot_ref[...])
    rope = split(rope_ref[...] * factor)
    for head in range(rope_ref_out.shape[0]):
        high, low = columns(rope, head * ROPE, ROPE)
        rope_ref_out[head, :, :] = jnp.concatenate([high, low, high], axis=1)


def attention_kernel(ways, chips, *refs):
    token_refs, refs = refs[:ways], refs[ways:]
    up_refs, refs = refs[: 2 * chips], refs[2 * chips :]
    mask_ref, rope_ref, nope_refs, cot_refs, refs = refs[0], refs[1], refs[2:4], refs[4:6], refs[6:]
    keep_refs, refs = refs[:chips], refs[chips:]
    send_ref, share_refs, refs = refs[0], refs[1 : 1 + ways], refs[1 + ways :]
    grad_scores_refs, key_rows_refs, shared_refs = refs[0:2], refs[2:4], refs[4:6]
    latent_all, shared_all, key_all, value_all, up_grad = refs[6:]
    length, width = nope_refs[0].shape
    lat = latent_all.shape[1]
    rows = length // ways
    rows_up = up_refs[0].shape[0] // 2
    head_count = width // NOPE
    mine, row = lax.axis_index("head"), lax.axis_index("fsdp")

    for step in range(ways):
        at = rows_at(partner(mine, step, ways), rows)
        block = token_refs[step][...]
        latent_all[at, :] = block[:rows, :]
        shared_all[at, :] = unpack_narrow(rows, lat, block)
    for step in range(2 * chips):
        at = rows_at(jnp.bitwise_xor(row, step), rows_up)
        key_all[at, :] = up_refs[step][:rows_up, :]
        value_all[at, :] = up_refs[step][rows_up:, :]

    latent = split(latent_all[...])
    shared = keep_pair(shared_refs, shared_all[...])
    key_up, value_up = split(key_all[...]), split(value_all[...])
    key_rows = keep_pair(key_rows_refs, product(latent, key_up, 1, 0))
    value_rows = split(product(latent, value_up, 1, 0))

    shared_parts = jnp.concatenate([shared[0], shared[0], shared[1]], axis=1)

    def front(head):
        nope, cot = columns(nope_refs, head * NOPE, NOPE), columns(cot_refs, head * VHEAD, VHEAD)
        keys, values = columns(key_rows, head * NOPE, NOPE), columns(value_rows, head * VHEAD, VHEAD)
        scores = joined_dot([*nope, nope[0], rope_ref[head]], [keys[0], *keys, shared_parts])
        return scores + mask_ref[...], joined_dot([*cot, cot[0]], [values[0], *values])

    def middle(head, scores, grad_attend):
        weight = jnp.exp(scores - jnp.max(scores, axis=1, keepdims=True))
        attend = weight * (1.0 / jnp.sum(weight, axis=1, keepdims=True))
        weighted = attend * grad_attend
        grad_scores = keep_pair(
            [ref.at[head] for ref in grad_scores_refs],
            weighted - attend * jnp.sum(weighted, axis=1, keepdims=True),
        )
        return split(attend), grad_scores

    def back(head, attend, grad_scores):
        nope, cot = columns(nope_refs, head * NOPE, NOPE), columns(cot_refs, head * VHEAD, VHEAD)
        rope = rope_ref[head][:, : 2 * ROPE]
        both_cot = over_rows(attend[0], jnp.concatenate(cot, axis=1))
        both_nope = over_rows(grad_scores[0], jnp.concatenate(nope, axis=1))
        low = over_rows(grad_scores[1], jnp.concatenate([nope[0], rope], axis=1))
        return (
            both_cot[:, :VHEAD] + both_cot[:, VHEAD:] + over_rows(attend[1], cot[0]),
            both_nope[:, :NOPE] + both_nope[:, NOPE:] + low[:, :NOPE],
            over_rows(grad_scores[0], rope) + low[:, NOPE:],
        )

    value_grads, key_grads = [], []
    shared_grad = jnp.zeros((length, 2 * ROPE), F32)
    ready = front(0)
    for head in range(head_count):
        later = front(head + 1) if head + 1 < head_count else None
        value_part, key_part, shared_part = back(head, *middle(head, *ready))
        value_grads.append(value_part)
        key_grads.append(key_part)
        shared_grad = shared_grad + shared_part
        ready = later
    key_grad = split(jnp.concatenate(key_grads, axis=1))
    value_grad = split(jnp.concatenate(value_grads, axis=1))

    latent_all[...] = product(key_grad, key_up, 1, 1) + product(value_grad, value_up, 1, 1)
    shared_all[...] = shared_grad[:, :ROPE] + shared_grad[:, ROPE:]
    for step in range(ways):
        at = rows_at(partner(mine, step, ways), rows)
        pack_tokens(rows, lat, share_refs[step], latent_all[at, :], shared_all[at, :])

    up_grad[:, :width] = product(latent, key_grad, 0, 0)
    up_grad[:, width:] = product(latent, value_grad, 0, 0)
    for step in range(chips):
        keep_refs[step][...] = up_grad[rows_at(jnp.bitwise_xor(row, 2 * step), rows_up), :]
        send_ref[step, :, :] = up_grad[rows_at(jnp.bitwise_xor(row, 2 * step + 1), rows_up), :]


def query_kernel(*refs):
    high_ref, low_ref = refs[:2]
    key_rows, shared = [(refs[2 * which][...], refs[2 * which + 1][...]) for which in (1, 2)]
    nope_out, rope_out = refs[6:]
    factor = (NOPE + ROPE) ** (-0.5)
    for head in range(high_ref.shape[0]):
        grad_scores = high_ref[head, :, :], low_ref[head, :, :]
        keys = columns(key_rows, head * NOPE, NOPE)
        nope_out[:, head * NOPE : (head + 1) * NOPE] = product(grad_scores, keys, 1, 0) * factor
        rope_out[:, head * ROPE : (head + 1) * ROPE] = product(grad_scores, shared, 1, 0) * factor


def join_kernel(chips, *refs):
    received, keep, outs = refs[0], refs[1 : 1 + chips], refs[1 + chips :]
    width = outs[0].shape[1]
    for step in range(chips):
        total = keep[step][...] + received[step, :, :]
        outs[step][...] = total[:, :width]
        outs[chips + step][...] = total[:, width:]


def add_kernel(*refs):
    count = len(refs) // 3
    for which in range(count):
        refs[2 * count + which][...] = refs[which][...] + refs[count + which][...]


def sum_kernel(counts, *refs):
    refs, outs, sums, sems = refs[: sum(counts)], refs[-9:-5], refs[-5:-1], refs[-1]
    latent_sum, rope_sum, key_sum, value_sum = sums
    copies = [pltpu.make_async_copy(src, out, sems.at[which]) for which, (src, out) in enumerate(zip(sums, outs))]

    def total(count):
        nonlocal refs
        value = refs[0][...]
        for ref in refs[1:count]:
            value = value + ref[...]
        refs = refs[count:]
        return value

    tokens = total(counts[0])
    rows, lat = latent_sum.shape
    latent_sum[...] = tokens[:rows, :]
    copies[0].start()
    key_sum[...] = total(counts[1])
    copies[2].start()
    value_sum[...] = total(counts[2])
    copies[3].start()
    rope_sum[...] = unpack_narrow(rows, lat, tokens)
    copies[1].start()
    for copy in copies:
        copy.wait()


def vmem(*arrays):
    return [pltpu.with_memory_space_constraint(array, pltpu.VMEM) for array in arrays]


def stored(*arrays):
    return [pltpu.with_memory_space_constraint(array, pltpu.HBM) for array in arrays]


def hbm(*dims):
    return pltpu.HBM(dims, F32)


def limit(mebibytes):
    return pltpu.CompilerParams(vmem_limit_bytes=mebibytes << 20)


def on_device(fsdp, ways, query_nope, query_rope, latent, rope_key, cotangent, bounds, key_up, value_up):
    chips = fsdp // 2
    rows, lat = latent.shape
    rows_up, width = key_up.shape
    length = query_nope.shape[0]
    packed = rows + rows * ROPE // lat
    dma = pltpu.SemaphoreType.DMA

    def swap(x, step):
        return lax.ppermute(x, "fsdp", [(i, i ^ step) for i in range(fsdp)])

    def shift(x, step):
        return lax.ppermute(x, "head", [(i, (i + step) % ways) for i in range(ways)])

    tokens, ups = pl.pallas_call(
        pack_kernel, out_shape=(pltpu.VMEM((packed, lat), F32), pltpu.VMEM((2 * rows_up, width), F32)),
        in_specs=[HBM] * 4, out_specs=[VMEM] * 2,
        scratch_shapes=[pltpu.VMEM((rows, ROPE), F32), dma((4,))],
        compiler_params=limit(4), name="pack",
    )(*stored(latent, rope_key, key_up, value_up))
    token_blocks = [tokens] + [shift(tokens, ways - step) for step in range(1, ways)]
    even = [ups] + [swap(ups, 2 * step) for step in range(1, chips)]
    odd = [swap(block, 1) for block in even]
    up_blocks = [block for pair in zip(even, odd) for block in pair]

    heads = width // NOPE
    wide, whole = (length, width), (lat, width)
    pairs = [(heads, length, length), wide, (length, ROPE)]
    queries = pl.pallas_call(
        prepare_kernel,
        out_shape=[pltpu.VMEM((length, length), F32)]
        + [pltpu.VMEM((heads, length, 3 * ROPE), BF16)] + [pltpu.VMEM(wide, BF16)] * 4,
        in_specs=[SMEM] + [VMEM] * 3, out_specs=[VMEM] * 6, compiler_params=limit(8), name="prepare",
    )(*stored(bounds, query_nope, query_rope, cotangent))
    out = pl.pallas_call(
        functools.partial(attention_kernel, ways, chips),
        out_shape=(
            *([pltpu.VMEM((rows_up, 2 * width), F32)] * chips), pltpu.VMEM((chips, rows_up, 2 * width), F32),
            *([pltpu.VMEM((packed, lat), F32)] * ways), *[pltpu.VMEM(dims, BF16) for dims in pairs for _ in range(2)],
        ),
        in_specs=[VMEM] * (ways + fsdp + 6),
        out_specs=[VMEM] * (chips + 1 + ways + 2 * len(pairs)),
        scratch_shapes=[
            pltpu.VMEM((length, lat), F32), pltpu.VMEM((length, ROPE), F32),
            pltpu.VMEM(whole, F32), pltpu.VMEM(whole, F32), pltpu.VMEM((lat, 2 * width), F32),
        ],
        compiler_params=limit(24), name="attention",
    )(*vmem(*token_blocks, *up_blocks, *queries))
    keep, send, shares, pairs = out[:chips], out[chips], out[chips + 1 : chips + 1 + ways], out[chips + 1 + ways :]

    nope_grad, rope_grad = pl.pallas_call(
        query_kernel, out_shape=(hbm(*wide), hbm(*query_rope.shape)),
        in_specs=[VMEM] * 6, out_specs=[VMEM] * 2, compiler_params=limit(8), name="query",
    )(*vmem(*pairs))

    block = pltpu.VMEM((rows_up, width), F32)
    received = swap(send, 1)
    joined = pl.pallas_call(
        functools.partial(join_kernel, chips), out_shape=[block] * (2 * chips),
        in_specs=[VMEM] * (1 + chips), out_specs=[VMEM] * (2 * chips), compiler_params=limit(6), name="join",
    )(*vmem(received, *keep))
    keys, values = list(joined[:chips]), list(joined[chips:])
    if square(chips):
        relayed = swap(keys[3], 2), swap(values[3], 4)
        direct = swap(keys[1], 2), swap(values[2], 4)
        added = pl.pallas_call(
            add_kernel, out_shape=[block] * 2, in_specs=[VMEM] * 4, out_specs=[VMEM] * 2,
            compiler_params=limit(4), name="relay",
        )(*vmem(keys[2], values[1], *relayed))
        key_parts = [keys[0], direct[0], swap(added[0], 4)]
        value_parts = [values[0], direct[1], swap(added[1], 2)]
    else:
        key_parts = keys[:1] + [swap(keys[step], 2 * step) for step in range(1, chips)]
        value_parts = values[:1] + [swap(values[step], 2 * step) for step in range(1, chips)]
    pieces = [shares[0]] + [shift(shares[step], step) for step in range(1, ways)]
    finals = [(rows, lat), (rows, ROPE), (rows_up, width), (rows_up, width)]
    counts = len(pieces), len(key_parts), len(value_parts)
    latent_grad, rope_key_grad, key_up_grad, value_up_grad = pl.pallas_call(
        functools.partial(sum_kernel, counts), out_shape=[hbm(*dims) for dims in finals],
        in_specs=[VMEM] * sum(counts), out_specs=[HBM] * 4,
        scratch_shapes=[pltpu.VMEM(dims, F32) for dims in finals] + [dma((4,))],
        compiler_params=limit(6), name="sums",
    )(*vmem(*pieces, *key_parts, *value_parts))
    return nope_grad, rope_grad, latent_grad, rope_key_grad, key_up_grad, value_up_grad


def solution(mesh):
    fsdp, ways = mesh.shape["fsdp"], mesh.shape["head"]

    def body(*args):
        return on_device(fsdp, ways, *args)

    return jax.shard_map(
        body,
        mesh=mesh,
        in_specs=(
            P("fsdp", "head"),
            P("fsdp", "head"),
            P(("fsdp", "head"), None),
            P(("fsdp", "head"), None),
            P("fsdp", "head"),
            P("fsdp", None),
            P("fsdp", "head"),
            P("fsdp", "head"),
        ),
        out_specs=(
            P("fsdp", "head"),
            P("fsdp", "head"),
            P(("fsdp", "head"), None),
            P(("fsdp", "head"), None),
            P("fsdp", "head"),
            P("fsdp", "head"),
        ),
        check_vma=False,
    )
```

```python
import functools

import jax
import jax.numpy as jnp
from jax import lax
from jax.experimental import pallas as pl
from jax.experimental.pallas import tpu as pltpu
from jax.sharding import PartitionSpec as P

NOPE = 128
ROPE = 64
VHEAD = 128
F32 = jnp.float32
BF16 = jnp.bfloat16


HBM = pl.BlockSpec(memory_space=pltpu.HBM)
VMEM = pl.BlockSpec(memory_space=pltpu.VMEM)
SMEM = pl.BlockSpec(memory_space=pltpu.SMEM)


def split(x):
    high = x.astype(BF16)
    return high, (x - high.astype(F32)).astype(BF16)


def product(left, right, left_dim, right_dim):
    dims = (((left_dim,), (right_dim,)), ((), ()))
    dot = functools.partial(lax.dot_general, dimension_numbers=dims, preferred_element_type=F32)
    return dot(left[0], right[0]) + (dot(left[0], right[1]) + dot(left[1], right[0]))


def joined_dot(left, right):
    left, right = jnp.concatenate(left, axis=1), jnp.concatenate(right, axis=1)
    return lax.dot_general(left, right, (((1,), (1,)), ((), ())), preferred_element_type=F32)


def over_rows(left, right):
    return lax.dot_general(left, right, (((0,), (0,)), ((), ())), preferred_element_type=F32)


def columns(pair, start, size):
    return pair[0][:, start : start + size], pair[1][:, start : start + size]


def keep_pair(refs, x):
    pair = split(x)
    refs[0][...], refs[1][...] = pair
    return pair


def square(chips):
    return chips == 4


def partner(mine, step, ways):
    return lax.rem(mine + step, ways)


def rows_at(index, rows):
    return pl.ds(pl.multiple_of(index * rows, 8), rows)


def pack_tokens(rows, lat, out_ref, wide, narrow):
    folds = lat // ROPE
    fold = rows // folds
    out_ref[:rows, :] = wide
    for part in range(folds):
        out_ref[rows : rows + fold, part * ROPE : (part + 1) * ROPE] = narrow[part * fold : (part + 1) * fold, :]


def unpack_narrow(rows, lat, block):
    folds = lat // ROPE
    fold = rows // folds
    return jnp.concatenate([block[rows : rows + fold, part * ROPE : (part + 1) * ROPE] for part in range(folds)], axis=0)


def pack_kernel(latent_ref, rope_ref, key_ref, value_ref, tokens_out, ups_out, rope, sems):
    rows, lat = latent_ref.shape
    rows_up = key_ref.shape[0]
    copies = [
        pltpu.make_async_copy(rope_ref, rope, sems.at[0]),
        pltpu.make_async_copy(key_ref, ups_out.at[pl.ds(0, rows_up)], sems.at[1]),
        pltpu.make_async_copy(value_ref, ups_out.at[pl.ds(rows_up, rows_up)], sems.at[2]),
        pltpu.make_async_copy(latent_ref, tokens_out.at[pl.ds(0, rows)], sems.at[3]),
    ]
    for copy in copies:
        copy.start()
    copies[0].wait()
    folds = lat // ROPE
    fold = rows // folds
    for part in range(folds):
        tokens_out[rows : rows + fold, part * ROPE : (part + 1) * ROPE] = rope[part * fold : (part + 1) * fold, :]
    for copy in copies[1:]:
        copy.wait()


def prepare_kernel(limit_ref, nope_ref, rope_ref, cot_ref, mask_ref, *refs):
    factor = (NOPE + ROPE) ** (-0.5)
    query_pos = lax.broadcasted_iota(jnp.int32, mask_ref.shape, 0)
    key_pos = lax.broadcasted_iota(jnp.int32, mask_ref.shape, 1)
    visible = (key_pos < limit_ref[0, 1]) & ((key_pos <= query_pos) | (key_pos < limit_ref[0, 0]))
    mask_ref[...] = jnp.where(visible, 0.0, -jnp.inf)
    rope_ref_out, nope_refs, cot_refs = refs[0], refs[1:3], refs[3:5]
    keep_pair(nope_refs, nope_ref[...] * factor)
    keep_pair(cot_refs, cot_ref[...])
    rope = split(rope_ref[...] * factor)
    for head in range(rope_ref_out.shape[0]):
        high, low = columns(rope, head * ROPE, ROPE)
        rope_ref_out[head, :, :] = jnp.concatenate([high, low, high], axis=1)


def attention_kernel(ways, chips, *refs):
    token_refs, refs = refs[:ways], refs[ways:]
    up_refs, refs = refs[: 2 * chips], refs[2 * chips :]
    mask_ref, rope_ref, nope_refs, cot_refs, refs = refs[0], refs[1], refs[2:4], refs[4:6], refs[6:]
    keep_refs, refs = refs[:chips], refs[chips:]
    send_ref, share_refs, refs = refs[0], refs[1 : 1 + ways], refs[1 + ways :]
    grad_scores_refs, key_rows_refs, shared_refs = refs[0:2], refs[2:4], refs[4:6]
    latent_all, shared_all, key_all, value_all, up_grad = refs[6:]
    length, width = nope_refs[0].shape
    lat = latent_all.shape[1]
    rows = length // ways
    rows_up = up_refs[0].shape[0] // 2
    head_count = width // NOPE
    mine, row = lax.axis_index("head"), lax.axis_index("fsdp")

    for step in range(ways):
        at = rows_at(partner(mine, step, ways), rows)
        block = token_refs[step][...]
        latent_all[at, :] = block[:rows, :]
        shared_all[at, :] = unpack_narrow(rows, lat, block)
    for step in range(2 * chips):
        at = rows_at(jnp.bitwise_xor(row, step), rows_up)
        key_all[at, :] = up_refs[step][:rows_up, :]
        value_all[at, :] = up_refs[step][rows_up:, :]

    latent = split(latent_all[...])
    shared = keep_pair(shared_refs, shared_all[...])
    key_up, value_up = split(key_all[...]), split(value_all[...])
    key_rows = keep_pair(key_rows_refs, product(latent, key_up, 1, 0))
    value_rows = split(product(latent, value_up, 1, 0))

    shared_parts = jnp.concatenate([shared[0], shared[0], shared[1]], axis=1)

    def front(head):
        nope, cot = columns(nope_refs, head * NOPE, NOPE), columns(cot_refs, head * VHEAD, VHEAD)
        keys, values = columns(key_rows, head * NOPE, NOPE), columns(value_rows, head * VHEAD, VHEAD)
        scores = joined_dot([*nope, nope[0], rope_ref[head]], [keys[0], *keys, shared_parts])
        return scores + mask_ref[...], joined_dot([*cot, cot[0]], [values[0], *values])

    def middle(head, scores, grad_attend):
        weight = jnp.exp(scores - jnp.max(scores, axis=1, keepdims=True))
        attend = weight * (1.0 / jnp.sum(weight, axis=1, keepdims=True))
        weighted = attend * grad_attend
        grad_scores = keep_pair(
            [ref.at[head] for ref in grad_scores_refs],
            weighted - attend * jnp.sum(weighted, axis=1, keepdims=True),
        )
        return split(attend), grad_scores

    def back(head, attend, grad_scores):
        nope, cot = columns(nope_refs, head * NOPE, NOPE), columns(cot_refs, head * VHEAD, VHEAD)
        rope = rope_ref[head][:, : 2 * ROPE]
        both_cot = over_rows(attend[0], jnp.concatenate(cot, axis=1))
        both_nope = over_rows(grad_scores[0], jnp.concatenate(nope, axis=1))
        low = over_rows(grad_scores[1], jnp.concatenate([nope[0], rope], axis=1))
        return (
            both_cot[:, :VHEAD] + both_cot[:, VHEAD:] + over_rows(attend[1], cot[0]),
            both_nope[:, :NOPE] + both_nope[:, NOPE:] + low[:, :NOPE],
            over_rows(grad_scores[0], rope) + low[:, NOPE:],
        )

    value_grads, key_grads = [], []
    shared_grad = jnp.zeros((length, 2 * ROPE), F32)
    fronts = [front(head) for head in range(head_count)]
    for head in range(head_count):
        value_part, key_part, shared_part = back(head, *middle(head, *fronts[head]))
        value_grads.append(value_part)
        key_grads.append(key_part)
        shared_grad = shared_grad + shared_part
    key_grad = split(jnp.concatenate(key_grads, axis=1))
    value_grad = split(jnp.concatenate(value_grads, axis=1))

    latent_all[...] = product(key_grad, key_up, 1, 1) + product(value_grad, value_up, 1, 1)
    shared_all[...] = shared_grad[:, :ROPE] + shared_grad[:, ROPE:]
    for step in range(ways):
        at = rows_at(partner(mine, step, ways), rows)
        pack_tokens(rows, lat, share_refs[step], latent_all[at, :], shared_all[at, :])

    up_grad[:, :width] = product(latent, key_grad, 0, 0)
    up_grad[:, width:] = product(latent, value_grad, 0, 0)
    for step in range(chips):
        keep_refs[step][...] = up_grad[rows_at(jnp.bitwise_xor(row, 2 * step), rows_up), :]
        send_ref[step, :, :] = up_grad[rows_at(jnp.bitwise_xor(row, 2 * step + 1), rows_up), :]


def query_kernel(*refs):
    high_ref, low_ref = refs[:2]
    key_rows, shared = [(refs[2 * which][...], refs[2 * which + 1][...]) for which in (1, 2)]
    nope_out, rope_out = refs[6:]
    factor = (NOPE + ROPE) ** (-0.5)
    for head in range(high_ref.shape[0]):
        grad_scores = high_ref[head, :, :], low_ref[head, :, :]
        keys = columns(key_rows, head * NOPE, NOPE)
        nope_out[:, head * NOPE : (head + 1) * NOPE] = product(grad_scores, keys, 1, 0) * factor
        rope_out[:, head * ROPE : (head + 1) * ROPE] = product(grad_scores, shared, 1, 0) * factor


def join_kernel(chips, *refs):
    received, keep, outs = refs[0], refs[1 : 1 + chips], refs[1 + chips :]
    width = outs[0].shape[1]
    for step in range(chips):
        total = keep[step][...] + received[step, :, :]
        outs[step][...] = total[:, :width]
        outs[chips + step][...] = total[:, width:]


def add_kernel(*refs):
    count = len(refs) // 3
    for which in range(count):
        refs[2 * count + which][...] = refs[which][...] + refs[count + which][...]


def sum_kernel(counts, *refs):
    refs, outs, sums, sems = refs[: sum(counts)], refs[-9:-5], refs[-5:-1], refs[-1]
    latent_sum, rope_sum, key_sum, value_sum = sums
    copies = [pltpu.make_async_copy(src, out, sems.at[which]) for which, (src, out) in enumerate(zip(sums, outs))]

    def total(count):
        nonlocal refs
        value = refs[0][...]
        for ref in refs[1:count]:
            value = value + ref[...]
        refs = refs[count:]
        return value

    tokens = total(counts[0])
    rows, lat = latent_sum.shape
    latent_sum[...] = tokens[:rows, :]
    copies[0].start()
    key_sum[...] = total(counts[1])
    copies[2].start()
    value_sum[...] = total(counts[2])
    copies[3].start()
    rope_sum[...] = unpack_narrow(rows, lat, tokens)
    copies[1].start()
    for copy in copies:
        copy.wait()


def vmem(*arrays):
    return [pltpu.with_memory_space_constraint(array, pltpu.VMEM) for array in arrays]


def stored(*arrays):
    return [pltpu.with_memory_space_constraint(array, pltpu.HBM) for array in arrays]


def hbm(*dims):
    return pltpu.HBM(dims, F32)


def limit(mebibytes):
    return pltpu.CompilerParams(vmem_limit_bytes=mebibytes << 20)


def on_device(fsdp, ways, query_nope, query_rope, latent, rope_key, cotangent, bounds, key_up, value_up):
    chips = fsdp // 2
    rows, lat = latent.shape
    rows_up, width = key_up.shape
    length = query_nope.shape[0]
    packed = rows + rows * ROPE // lat
    dma = pltpu.SemaphoreType.DMA

    def swap(x, step):
        return lax.ppermute(x, "fsdp", [(i, i ^ step) for i in range(fsdp)])

    def shift(x, step):
        return lax.ppermute(x, "head", [(i, (i + step) % ways) for i in range(ways)])

    tokens, ups = pl.pallas_call(
        pack_kernel, out_shape=(pltpu.VMEM((packed, lat), F32), pltpu.VMEM((2 * rows_up, width), F32)),
        in_specs=[HBM] * 4, out_specs=[VMEM] * 2,
        scratch_shapes=[pltpu.VMEM((rows, ROPE), F32), dma((4,))],
        compiler_params=limit(4), name="pack",
    )(*stored(latent, rope_key, key_up, value_up))
    token_blocks = [tokens] + [shift(tokens, ways - step) for step in range(1, ways)]
    even = [ups] + [swap(ups, 2 * step) for step in range(1, chips)]
    odd = [swap(block, 1) for block in even]
    up_blocks = [block for pair in zip(even, odd) for block in pair]

    heads = width // NOPE
    wide, whole = (length, width), (lat, width)
    pairs = [(heads, length, length), wide, (length, ROPE)]
    queries = pl.pallas_call(
        prepare_kernel,
        out_shape=[pltpu.VMEM((length, length), F32)]
        + [pltpu.VMEM((heads, length, 3 * ROPE), BF16)] + [pltpu.VMEM(wide, BF16)] * 4,
        in_specs=[SMEM] + [VMEM] * 3, out_specs=[VMEM] * 6, compiler_params=limit(8), name="prepare",
    )(*stored(bounds, query_nope, query_rope, cotangent))
    out = pl.pallas_call(
        functools.partial(attention_kernel, ways, chips),
        out_shape=(
            *([pltpu.VMEM((rows_up, 2 * width), F32)] * chips), pltpu.VMEM((chips, rows_up, 2 * width), F32),
            *([pltpu.VMEM((packed, lat), F32)] * ways), *[pltpu.VMEM(dims, BF16) for dims in pairs for _ in range(2)],
        ),
        in_specs=[VMEM] * (ways + fsdp + 6),
        out_specs=[VMEM] * (chips + 1 + ways + 2 * len(pairs)),
        scratch_shapes=[
            pltpu.VMEM((length, lat), F32), pltpu.VMEM((length, ROPE), F32),
            pltpu.VMEM(whole, F32), pltpu.VMEM(whole, F32), pltpu.VMEM((lat, 2 * width), F32),
        ],
        compiler_params=limit(24), name="attention",
    )(*vmem(*token_blocks, *up_blocks, *queries))
    keep, send, shares, pairs = out[:chips], out[chips], out[chips + 1 : chips + 1 + ways], out[chips + 1 + ways :]

    nope_grad, rope_grad = pl.pallas_call(
        query_kernel, out_shape=(hbm(*wide), hbm(*query_rope.shape)),
        in_specs=[VMEM] * 6, out_specs=[VMEM] * 2, compiler_params=limit(8), name="query",
    )(*vmem(*pairs))

    block = pltpu.VMEM((rows_up, width), F32)
    received = swap(send, 1)
    joined = pl.pallas_call(
        functools.partial(join_kernel, chips), out_shape=[block] * (2 * chips),
        in_specs=[VMEM] * (1 + chips), out_specs=[VMEM] * (2 * chips), compiler_params=limit(6), name="join",
    )(*vmem(received, *keep))
    keys, values = list(joined[:chips]), list(joined[chips:])
    if square(chips):
        relayed = swap(keys[3], 2), swap(values[3], 4)
        direct = swap(keys[1], 2), swap(values[2], 4)
        added = pl.pallas_call(
            add_kernel, out_shape=[block] * 2, in_specs=[VMEM] * 4, out_specs=[VMEM] * 2,
            compiler_params=limit(4), name="relay",
        )(*vmem(keys[2], values[1], *relayed))
        key_parts = [keys[0], direct[0], swap(added[0], 4)]
        value_parts = [values[0], direct[1], swap(added[1], 2)]
    else:
        key_parts = keys[:1] + [swap(keys[step], 2 * step) for step in range(1, chips)]
        value_parts = values[:1] + [swap(values[step], 2 * step) for step in range(1, chips)]
    pieces = [shares[0]] + [shift(shares[step], step) for step in range(1, ways)]
    finals = [(rows, lat), (rows, ROPE), (rows_up, width), (rows_up, width)]
    counts = len(pieces), len(key_parts), len(value_parts)
    latent_grad, rope_key_grad, key_up_grad, value_up_grad = pl.pallas_call(
        functools.partial(sum_kernel, counts), out_shape=[hbm(*dims) for dims in finals],
        in_specs=[VMEM] * sum(counts), out_specs=[HBM] * 4,
        scratch_shapes=[pltpu.VMEM(dims, F32) for dims in finals] + [dma((4,))],
        compiler_params=limit(6), name="sums",
    )(*vmem(*pieces, *key_parts, *value_parts))
    return nope_grad, rope_grad, latent_grad, rope_key_grad, key_up_grad, value_up_grad


def solution(mesh):
    fsdp, ways = mesh.shape["fsdp"], mesh.shape["head"]

    def body(*args):
        return on_device(fsdp, ways, *args)

    return jax.shard_map(
        body,
        mesh=mesh,
        in_specs=(
            P("fsdp", "head"),
            P("fsdp", "head"),
            P(("fsdp", "head"), None),
            P(("fsdp", "head"), None),
            P("fsdp", "head"),
            P("fsdp", None),
            P("fsdp", "head"),
            P("fsdp", "head"),
        ),
        out_specs=(
            P("fsdp", "head"),
            P("fsdp", "head"),
            P(("fsdp", "head"), None),
            P(("fsdp", "head"), None),
            P("fsdp", "head"),
            P("fsdp", "head"),
        ),
        check_vma=False,
    )
```
